512 devices in a mesh: src: 16 (over y, x_hi), space: 32 (over x_lo, z, core).
Axes of the slice: x: 4 (x_hi: 2, x_lo: 2; x = x_hi * 2 + x_lo), y: 8, z: 8, core: 2. Of those that a mesh axis runs over, the one named last changes fastest.
Arguments:
- velocity: float32 [32, 512, 256], P('space'), may hold values from 0.5 to 2
- station_cells: int32 [16, 3], P('src'), may hold values from 0 to 511, as said below
- event_cells: int32 [3, 8192], replicated, may hold values from 0 to 511, as said below
- delays: float32 [16, 8192], P('src'), may hold values from -6 to 6
- active: int32 [2, 16, 32, 16], P(None, 'src', 'space'), may hold values from 0 to 1, as said below
Outputs:
- traveltimes: float32 [16, 32, 512, 256], P('src', 'space')
- kernel: float32 [32, 512, 256], P('space', 'src')
The draws below stay inside these ranges and needn't reach their ends.
Inputs may be any that keep to these rules, and one draw needn't show every extreme that they name: `station_cells`: stations lie in the top four layers: third coordinate below 4, first below 32, second below 512. `event_cells`: row 0 holds first coordinates below 32, row 1 second ones below 512, row 2 third ones below 256. `active`: 1 marks a tile whose cells are updated in that round for that station.
All inputs are finite; a program needn't handle non-finite values.
Results may differ from the reference program's by a relative error of at most 0.0003.
Values sent between devices are 32-bit elements; how exact they have to be, the bound alone decides.
A program may use at most 64 MiB of HBM per device.

```python
import math
import jax
import jax.numpy as jnp
from jax import lax

CX = 1
NY = 512
NZ = 256
TY = 32
ROUNDS = 2
SWEEPS = 2
ADJ_SWEEPS = 4
SOURCES = 16
NX = 32
EVENTS = 8192
NTX = 32
TILES = 16


def station_helper(key):
    inner = jax.random.fold_in(key, 11)
    key_x, key_y, key_z = jax.random.split(inner, 3)
    station_x = jax.random.randint(key_x, (SOURCES,), 0, NX)
    station_y = jax.random.randint(key_y, (SOURCES,), 0, NY)
    station_z = jax.random.randint(key_z, (SOURCES,), 0, 4)
    station_x = station_x.at[0].set(NX - 1).at[1].set(0)
    station_y = station_y.at[0].set(NY - 1).at[1].set(0)
    station_z = station_z.at[0].set(0).at[1].set(0)
    return jnp.stack([station_x, station_y, station_z], axis=1).astype(jnp.int32)


def draw_station_cells(key, part):
    return station_helper(key)


def draw_event_cells(key, part):
    inner = jax.random.fold_in(key, 37)
    key_x, key_y, key_z = jax.random.split(inner, 3)
    event_x = jax.random.randint(key_x, (EVENTS,), 0, NX)
    event_y = jax.random.randint(key_y, (EVENTS,), 0, NY)
    event_z = jax.random.randint(key_z, (EVENTS,), 0, NZ)
    event_x = event_x.at[0].set(NX - 1).at[1].set(0)
    event_y = event_y.at[0].set(NY - 1).at[1].set(0)
    event_z = event_z.at[0].set(NZ - 1).at[1].set(0)
    return jnp.stack([event_x, event_y, event_z], axis=0).astype(jnp.int32)


def draw_active(key, part):
    stations = station_helper(key)
    tile_x = stations[:, 0] // CX
    inner = jax.random.fold_in(key, 23)
    rolls = jax.random.randint(inner, (ROUNDS, SOURCES, NTX, TILES), 0, 4)
    tiles = jnp.arange(NTX, dtype=jnp.int32)
    reach = max(NTX // 4, 1)
    near = jnp.abs(tiles[None, :] - tile_x[:, None]) <= reach
    level = jnp.where(near, 3, 1)[None, :, :, None]
    return (rolls < level).astype(jnp.int32)


def shard_levels(stream_key, dims, cuts, low, top_value):
    def one(position, shards_of):
        draws = jax.random.uniform(jax.random.fold_in(jax.random.fold_in(stream_key, 6), position), (shards_of,), jnp.float32, low / len(cuts), top_value / len(cuts))
        return jnp.repeat(jnp.exp(draws), dims[position] // shards_of).reshape((-1,) + (1,) * (len(dims) - position - 1))

    loudness = one(*cuts[0])
    for cut in cuts[1:]:
        loudness = loudness * one(*cut)
    return loudness


def gaussian(stream_key, extent, spread, bound, pieces=(), kind=jnp.bfloat16):
    entries = spread * jax.random.normal(stream_key, extent, jnp.float32)
    if pieces:
        entries = entries * shard_levels(stream_key, extent, pieces, -0.22, 0.18)
    return jnp.clip(entries, -bound, bound).astype(kind)


def setup_inputs(seed: int = 0) -> dict:
    keys = jax.random.split(jax.random.key(seed), 6)
    velocity = jnp.clip(jnp.exp(math.log(2.0) - 1.3862944 * jax.random.uniform(keys[0], (NX, NY, NZ), jnp.float32) ** shard_levels(keys[0], (NX, NY, NZ), ((0, 32),), -0.2, 0.2)), 0.5, 2.0)
    station_cells = draw_station_cells(jax.random.fold_in(keys[5], 71), 0)
    event_cells = draw_event_cells(jax.random.fold_in(keys[5], 71), 0)
    delays = gaussian(keys[3], (SOURCES, EVENTS), 1.0, 6.0, ((0, 16),), jnp.float32)
    active = draw_active(jax.random.fold_in(keys[5], 71), 0)
    return {"velocity": velocity, "station_cells": station_cells, "event_cells": event_cells, "delays": delays, "active": active}


BIG = 1000000.0

def godunov(near_x, near_y, near_z, cost_cell):
    lowest = jnp.minimum(jnp.minimum(near_x, near_y), near_z)
    highest = jnp.maximum(jnp.maximum(near_x, near_y), near_z)
    middle = jnp.maximum(jnp.minimum(near_x, near_y), jnp.minimum(jnp.maximum(near_x, near_y), near_z))
    first_gap = middle - lowest
    second_gap = highest - lowest
    single = lowest + cost_cell
    double = lowest + 0.5 * (first_gap + jnp.sqrt(jnp.maximum(2.0 * cost_cell * cost_cell - first_gap * first_gap, 0.0)))
    gaps = first_gap + second_gap
    triple = lowest + (gaps + jnp.sqrt(jnp.maximum(gaps * gaps - 3.0 * (first_gap * first_gap + second_gap * second_gap - cost_cell * cost_cell), 0.0))) / 3.0
    return jnp.where(single <= middle, single, jnp.where(double <= highest, double, triple))

def neighbours(field, fill):
    padded = jnp.pad(field, 1, constant_values=fill)
    return [padded[:-2, 1:-1, 1:-1], padded[2:, 1:-1, 1:-1], padded[1:-1, :-2, 1:-1], padded[1:-1, 2:, 1:-1], padded[1:-1, 1:-1, :-2], padded[1:-1, 1:-1, 2:]]

def smooth_along(extended, axis_index):
    length = extended.shape[axis_index]
    first = lax.slice_in_dim(extended, 0, length - 2, axis=axis_index)
    centre = lax.slice_in_dim(extended, 1, length - 1, axis=axis_index)
    after = lax.slice_in_dim(extended, 2, length, axis=axis_index)
    return (first + 2.0 * centre + after) * 0.25

def pad_zero(field, axis_index):
    widths = [(0, 0)] * field.ndim
    widths[axis_index] = (1, 1)
    return jnp.pad(field, widths)

def reference(velocity, station_cells, event_cells, delays, active):
    slowness = 1.0 / velocity
    grid_x = lax.broadcasted_iota(jnp.int32, (NX, NY, NZ), 0)
    grid_y = lax.broadcasted_iota(jnp.int32, (NX, NY, NZ), 1)
    grid_z = lax.broadcasted_iota(jnp.int32, (NX, NY, NZ), 2)
    event_x = event_cells[0]
    event_y = event_cells[1]
    event_z = event_cells[2]
    flat_index = (event_x * (NY * NZ) + event_y * NZ + event_z).astype(jnp.int32)

    def station_solve(carry, inputs):
        station, delay_row, active_rows = inputs
        station_x = station[0]
        station_y = station[1]
        station_z = station[2]
        diff_x = (grid_x - station_x).astype(jnp.float32)
        diff_y = (grid_y - station_y).astype(jnp.float32)
        diff_z = (grid_z - station_z).astype(jnp.float32)
        times = jnp.sqrt(diff_x * diff_x + diff_y * diff_y + diff_z * diff_z)
        station_mask = (grid_x == station_x) & (grid_y == station_y) & (grid_z == station_z)
        for round_index in range(ROUNDS):
            tile_mask = (active_rows[round_index] > 0)[:, None, :, None, None]
            for sweep in range(SWEEPS):
                beside_all = neighbours(times, BIG)
                update = godunov(jnp.minimum(beside_all[0], beside_all[1]), jnp.minimum(beside_all[2], beside_all[3]), jnp.minimum(beside_all[4], beside_all[5]), slowness)
                chosen = jnp.where(tile_mask, update.reshape(NX // CX, CX, NY // TY, TY, NZ), times.reshape(NX // CX, CX, NY // TY, TY, NZ)).reshape(NX, NY, NZ)
                times = jnp.where(station_mask, 0.0, chosen)
        picked = times.reshape(-1)[flat_index]
        event_dx = (event_x - station_x).astype(jnp.float32)
        event_dy = (event_y - station_y).astype(jnp.float32)
        event_dz = (event_z - station_z).astype(jnp.float32)
        direct = jnp.sqrt(event_dx * event_dx + event_dy * event_dy + event_dz * event_dz)
        misfit = picked - direct - delay_row
        source = jnp.zeros((NX * NY * NZ,), jnp.float32).at[flat_index].add(misfit).reshape(NX, NY, NZ)
        weights = [jnp.maximum(neighbour - times, 0.0) * velocity / 6.0 for neighbour in neighbours(times, BIG)]
        adjoint = source
        for sweep in range(ADJ_SWEEPS):
            summed = source
            for weight, neighbour in zip(weights, neighbours(adjoint, 0.0)):
                summed = summed + weight * neighbour
            adjoint = summed
        return (carry + adjoint, times)
    start = jnp.zeros((NX, NY, NZ), jnp.float32)
    adjoint_sum, travel = lax.scan(station_solve, start, (station_cells, delays, jnp.transpose(active, (1, 0, 2, 3))))
    density = slowness * adjoint_sum
    along_x = smooth_along(pad_zero(density, 0), 0)
    along_y = smooth_along(pad_zero(along_x, 1), 1)
    kernel = smooth_along(pad_zero(along_y, 2), 2)
    return (travel, kernel)
```

```python
import functools

import jax
import jax.numpy as jnp
from jax import lax
from jax.experimental import pallas as pl
from jax.experimental.pallas import tpu as pltpu
from jax.sharding import PartitionSpec as P

TY = 32
BIG = 1000000.0
HALO = 8
GROUP = 2
MESH = pl.DeviceIdType.MESH


def godunov(near_x, near_y, near_z, cost):
    low_xy = jnp.minimum(near_x, near_y)
    high_xy = jnp.maximum(near_x, near_y)
    lowest = jnp.minimum(low_xy, near_z)
    rest = jnp.maximum(low_xy, near_z)
    middle = jnp.minimum(high_xy, rest)
    highest = jnp.maximum(high_xy, rest)
    gap2 = middle - lowest
    gap3 = highest - lowest
    cost_sq = cost * cost
    gap2_sq = gap2 * gap2
    disc2 = 2.0 * cost_sq - gap2_sq
    reach = gap3 + gap3 - gap2
    two = disc2 <= reach * reach
    step = gap3 - gap2
    disc3 = 3.0 * cost_sq - (gap2_sq + gap3 * gap3 + step * step)
    disc = jnp.where(two, disc2, disc3)
    base = jnp.where(two, gap2, gap2 + gap3)
    scale = jnp.where(two, 0.5, 1.0 / 3.0)
    wide = lowest + (base + jnp.sqrt(jnp.maximum(disc, 0.0))) * scale
    return jnp.where(cost <= gap2, lowest + cost, wide)


def beside(field, axis):
    length = field.shape[axis]
    return pltpu.roll(field, 1, axis), pltpu.roll(field, length - 1, axis)


def kernel(
    dims,
    velocity_ref,
    meta_ref,
    events_ref,
    delays_ref,
    times_out,
    kernel_out,
    vel,
    slow,
    meta,
    delay,
    start,
    time_a,
    time_b,
    count,
    late,
    masks,
    spot,
    weights,
    adj_a,
    adj_b,
    dens,
    part,
    parts,
    total,
    send_sem,
    recv_sem,
    last_sem,
):
    n_src, n_space, ny, nz, events = dims
    group = GROUP
    rows = ny // (n_space * group)
    peers = n_src // group
    chunk_x = n_space // peers
    own_rows = ny // n_src
    per_owner = own_rows // rows
    tall = rows + 2 * HALO
    s, p = lax.axis_index("src"), lax.axis_index("space")
    m, g = s // group, s % group
    block = g * n_space + p
    y_base = block * rows
    n_blocks = n_space * group

    def where_is(b):
        return (m * group + b // n_space, b % n_space)

    owner = block // per_owner
    targets = [(owner, chunk_x * m + k) for k in range(chunk_x)]
    sources = []
    for k in range(per_owner):
        b = s * per_owner + k
        sources.append(((p // chunk_x) * group + b // n_space, b % n_space))

    barrier = pltpu.get_barrier_semaphore()
    signals = 0
    for dg in range(group):
        for i in range(n_space):
            if dg or i:
                to = (m * group + (g + dg) % group, (p + i) % n_space)
                pl.semaphore_signal(barrier, inc=1, device_id=to, device_id_type=MESH)
                signals += 1
    for i in range(1, peers):
        to = (((m + i) % peers) * group + g, p)
        pl.semaphore_signal(barrier, inc=1, device_id=to, device_id_type=MESH)
        signals += 1
    for to in sources:
        mine = (to[0] == s) & (to[1] == p)

        @pl.when(jnp.logical_not(mine))
        def _():
            pl.semaphore_signal(barrier, inc=1, device_id=to, device_id_type=MESH)

        signals = signals + jnp.where(mine, 0, 1)
    pl.semaphore_wait(barrier, signals)

    own = pl.ds(HALO, rows)
    for i in range(n_space):
        q = (p + i) % n_space
        piece = velocity_ref.at[pl.ds(pl.multiple_of((g * n_space + q) * rows, 8), rows), :]
        if i == 0:
            pltpu.make_async_copy(piece, vel.at[own, p, :], recv_sem.at[0]).start()
        else:
            pltpu.make_async_remote_copy(
                piece,
                vel.at[own, p, :],
                send_sem.at[0],
                recv_sem.at[0],
                device_id=(s, q),
                device_id_type=MESH,
            ).start()
    for dg in range(group):
        for i in range(n_space):
            line = meta.at[g, pl.ds(p, 1), :]
            if dg == 0 and i == 0:
                pltpu.make_async_copy(meta_ref, line, recv_sem.at[1]).start()
            else:
                to = (m * group + (g + dg) % group, (p + i) % n_space)
                pltpu.make_async_remote_copy(
                    meta_ref,
                    line,
                    send_sem.at[1],
                    recv_sem.at[1],
                    device_id=to,
                    device_id_type=MESH,
                ).start()
    for dg in range(group):
        if dg == 0:
            pltpu.make_async_copy(delays_ref, delay.at[g], recv_sem.at[2]).start()
        else:
            pltpu.make_async_remote_copy(
                delays_ref,
                delay.at[g],
                send_sem.at[2],
                recv_sem.at[2],
                device_id=(m * group + (g + dg) % group, p),
                device_id_type=MESH,
            ).start()
    pltpu.make_async_copy(delay, delay, recv_sem.at[2]).wait()

    src_rows = rows + 10
    cells = src_rows * n_space
    step_events = 1024
    count[...] = jnp.zeros_like(count)
    late[...] = jnp.zeros_like(late)

    def add_events(c, carry):
        at = pl.ds(pl.multiple_of(c * step_events, step_events), step_events)
        event_x = events_ref[0:1, at]
        event_y = events_ref[1:2, at]
        event_z = events_ref[2:3, at]
        key = (event_y - (y_base - 5)) * n_space + event_x
        cell = lax.broadcasted_iota(jnp.int32, (cells, step_events), 0)
        left = jnp.where(cell == key, 1.0, 0.0).astype(jnp.bfloat16)
        deep = lax.broadcasted_iota(jnp.int32, (nz, step_events), 0) == event_z
        contract = (((1,), (1,)), ((), ()))

        def product(value):
            right = jnp.where(deep, value, 0.0).astype(jnp.bfloat16)
            return lax.dot_general(left, right, contract, preferred_element_type=jnp.float32)

        count[...] += product(1.0)
        for k in range(group):
            lateness = delay[k, 0:1, at]
            coarse = lateness.astype(jnp.bfloat16).astype(jnp.float32)
            late[k] += product(coarse) + product(lateness - coarse)
        return carry

    lax.fori_loop(0, events // step_events, add_events, 0)

    pltpu.make_async_copy(meta, meta, recv_sem.at[1]).wait()
    lane = lax.broadcasted_iota(jnp.int32, (n_space, 128), 1)
    layer = lax.broadcasted_iota(jnp.int32, (n_space, nz), 0)
    depth = lax.broadcasted_iota(jnp.int32, (n_space, nz), 1)
    layer_f = layer.astype(jnp.float32)
    depth_f = depth.astype(jnp.float32)
    first_tile = (y_base - HALO + TY) // TY - 1
    tiles = ny // TY

    def column(k, index):
        picked = jnp.where(lane == index, meta[k], 0.0)
        return jnp.broadcast_to(jnp.sum(picked, axis=1, keepdims=True), (n_space, nz))

    def row_valid(y):
        return (y >= 0) & (y < ny)

    for k in range(group):
        for r in range(2):
            for t in range(2):
                masks[r, k, t] = column(k, r * tiles + first_tile + t)
            masks[r, k, 2] = jnp.zeros((n_space, nz), jnp.float32)
        cell_x, cell_y, cell_z = column(k, 64), column(k, 65), column(k, 66)
        here = (layer_f == cell_x) & (depth_f == cell_z)
        spot[k] = jnp.where(here, cell_y, -1.0)
        flat = (layer_f - cell_x) * (layer_f - cell_x) + (depth_f - cell_z) * (depth_f - cell_z)

        def init_row(j, carry):
            y = y_base - HALO - 1 + j
            diff = y.astype(jnp.float32) - cell_y
            start[k, j] = jnp.where(row_valid(y), jnp.sqrt(flat + diff * diff), BIG)
            return carry

        lax.fori_loop(0, tall + 2, init_row, 0)
        time_a[k, 0] = start[k, 0]

    pltpu.make_async_copy(vel.at[own], vel.at[own], recv_sem.at[0]).wait()
    before = where_is((block + n_blocks - 1) % n_blocks)
    after = where_is((block + 1) % n_blocks)
    to_before = pltpu.make_async_remote_copy(
        vel.at[pl.ds(HALO, HALO)],
        vel.at[pl.ds(HALO + rows, HALO)],
        send_sem.at[3],
        recv_sem.at[3],
        device_id=before,
        device_id_type=MESH,
    )
    to_after = pltpu.make_async_remote_copy(
        vel.at[pl.ds(rows, HALO)],
        vel.at[pl.ds(0, HALO)],
        send_sem.at[4],
        recv_sem.at[4],
        device_id=after,
        device_id_type=MESH,
    )
    to_before.start()
    to_after.start()
    to_before.wait_recv()
    to_after.wait_recv()

    def slow_row(j, carry):
        slow[j] = 1.0 / vel[j]
        return carry

    lax.fori_loop(0, tall, slow_row, 0)

    def sweep(k, source, target, low, high, r):
        def row(j, carry):
            y = y_base - HALO + j
            centre = source[k, j + 1]
            near_y = jnp.minimum(source[k, j], source[k, j + 2])
            x_low, x_high = beside(centre, 0)
            x_low = jnp.where(layer == 0, BIG, x_low)
            x_high = jnp.where(layer == n_space - 1, BIG, x_high)
            z_low, z_high = beside(centre, 1)
            z_low = jnp.where(depth == 0, BIG, z_low)
            z_high = jnp.where(depth == nz - 1, BIG, z_high)
            update = godunov(
                jnp.minimum(x_low, x_high), near_y, jnp.minimum(z_low, z_high), slow[j]
            )
            kind = jnp.where(row_valid(y), (y + TY) // TY - 1 - first_tile, 2)
            chosen = (masks[r, k, kind] > 0.0) & (spot[k] != y.astype(jnp.float32))
            target[k, j + 1] = jnp.where(chosen, update, centre)
            return carry

        lax.fori_loop(low, high, row, 0)

    inner = pl.ds(HALO + 1, rows)
    for k in range(group):
        sweep(k, start, time_a, 0, tall, 0)
        sweep(k, time_a, time_b, 1, tall - 1, 0)
        sweep(k, time_b, time_a, 2, tall - 2, 1)
        sweep(k, time_a, time_b, 3, tall - 3, 1)
        for i in range(n_space):
            q = (p + i) % n_space
            piece = time_b.at[k, inner, q, :]
            place = times_out.at[pl.ds(pl.multiple_of(y_base, 8), rows), :]
            to_src = m * group + k

            def send(piece=piece, place=place, to_src=to_src, q=q):
                pltpu.make_async_remote_copy(
                    piece,
                    place,
                    send_sem.at[5],
                    recv_sem.at[5],
                    device_id=(to_src, q),
                    device_id_type=MESH,
                ).start()

            if i:
                send()
            else:

                @pl.when(g == k)
                def _():
                    pltpu.make_async_copy(piece, place, recv_sem.at[5]).start()

                @pl.when(g != k)
                def _():
                    send()

    dens[...] = jnp.zeros_like(dens)
    for k in range(group):

        def source_row(i, carry):
            j = i + 3
            at = pl.ds(pl.multiple_of(i * n_space, n_space), n_space)
            value = count[at, :] * (time_b[k, j + 1] - start[k, j + 1]) - late[k, at, :]
            adj_a[0, i] = value
            adj_a[1, i] = value
            return carry

        lax.fori_loop(0, src_rows, source_row, 0)

        def weight_row(i, carry):
            j = i + 4
            centre = time_b[k, j + 1]
            rate = vel[j] * (1.0 / 6.0)
            x_low, x_high = beside(centre, 0)
            z_low, z_high = beside(centre, 1)
            around = (
                jnp.where(layer == 0, centre, x_low),
                jnp.where(layer == n_space - 1, centre, x_high),
                time_b[k, j],
                time_b[k, j + 2],
                jnp.where(depth == 0, centre, z_low),
                jnp.where(depth == nz - 1, centre, z_high),
            )
            for d, near in enumerate(around):
                weights[d, i] = jnp.maximum(near - centre, 0.0) * rate
            return carry

        lax.fori_loop(0, src_rows - 2, weight_row, 0)

        def adjoint_sweep(old, new, low, high):
            def row(i, carry):
                centre = old[i]
                x_low, x_high = beside(centre, 0)
                z_low, z_high = beside(centre, 1)
                value = adj_a[0, i]
                around = (x_low, x_high, old[i - 1], old[i + 1], z_low, z_high)
                for d, near in enumerate(around):
                    value = value + weights[d, i - 1] * near
                new[i] = value
                return carry

            lax.fori_loop(low, high, row, 0)

        adjoint_sweep(adj_a.at[1], adj_b, 1, src_rows - 1)
        adjoint_sweep(adj_b, adj_a.at[1], 2, src_rows - 2)
        adjoint_sweep(adj_a.at[1], adj_b, 3, src_rows - 3)
        adjoint_sweep(adj_b, adj_a.at[1], 4, src_rows - 4)

        def density_row(i, carry):
            dens[i] += slow[i + HALO - 1] * adj_a[1, i + 4]
            return carry

        lax.fori_loop(0, rows + 2, density_row, 0)

    def smooth_row(i, carry):
        value = dens[i] + 2.0 * dens[i + 1] + dens[i + 2]
        x_low, x_high = beside(value, 0)
        x_low = jnp.where(layer == 0, 0.0, x_low)
        x_high = jnp.where(layer == n_space - 1, 0.0, x_high)
        value = x_low + 2.0 * value + x_high
        z_low, z_high = beside(value, 1)
        z_low = jnp.where(depth == 0, 0.0, z_low)
        z_high = jnp.where(depth == nz - 1, 0.0, z_high)
        part[i] = (z_low + 2.0 * value + z_high) * (1.0 / 64.0)
        return carry

    lax.fori_loop(0, rows, smooth_row, 0)

    for i in range(peers):
        q = (m + i) % peers
        piece = part.at[:, pl.ds(pl.multiple_of(q * chunk_x, chunk_x), chunk_x), :]
        if i == 0:
            pltpu.make_async_copy(piece, parts.at[m], recv_sem.at[6]).start()
        else:
            pltpu.make_async_remote_copy(
                piece,
                parts.at[m],
                send_sem.at[6],
                recv_sem.at[6],
                device_id=(q * group + g, p),
                device_id_type=MESH,
            ).start()
    pltpu.make_async_copy(parts, parts, recv_sem.at[6]).wait()
    summed = parts[0]
    for i in range(1, peers):
        summed = summed + parts[i]
    total[...] = summed
    place_k = block % per_owner
    for k in range(chunk_x):
        to = targets[k]
        piece = total.at[:, k, :]
        place = kernel_out.at[pl.ds(pl.multiple_of(place_k * rows, 8), rows), :]
        mine = (to[0] == s) & (to[1] == p)

        @pl.when(mine)
        def _():
            pltpu.make_async_copy(piece, place, recv_sem.at[7]).start()

        @pl.when(jnp.logical_not(mine))
        def _():
            pltpu.make_async_remote_copy(
                piece,
                place,
                last_sem.at[k],
                recv_sem.at[7],
                device_id=to,
                device_id_type=MESH,
            ).start()

    def drain(ref, sem):
        pltpu.make_async_copy(ref, ref, sem).wait()

    for k in range(chunk_x):
        to = targets[k]
        mine = (to[0] == s) & (to[1] == p)

        @pl.when(jnp.logical_not(mine))
        def _():
            drain(total.at[:, k, :], last_sem.at[k])

    drain(velocity_ref.at[pl.ds(0, (n_space - 1) * rows), :], send_sem.at[0])
    for k in range(group):
        if k:
            drain(meta.at[k], send_sem.at[1])
        else:
            drain(meta.at[k, pl.ds(0, n_space - 8), :], send_sem.at[1])
            for _ in range(7):
                drain(meta_ref, send_sem.at[1])
    if group > 1:
        drain(delay.at[pl.ds(1, group - 1)], send_sem.at[2])
    to_before.wait_send()
    to_after.wait_send()
    drain(times_out.at[pl.ds(0, (n_blocks - 1) * rows), :], send_sem.at[5])
    drain(parts.at[pl.ds(1, peers - 1)], send_sem.at[6])
    drain(times_out, recv_sem.at[5])
    drain(kernel_out, recv_sem.at[7])


def per_device(dims, velocity, station_cells, event_cells, delays, active):
    n_src, n_space, ny, nz, events = dims
    rows = ny // (n_space * GROUP)
    tall = rows + 2 * HALO
    peers = n_src // GROUP
    chunk_x = n_space // peers
    own_rows = ny // n_src
    src_rows = rows + 10
    flags = active.reshape(1, -1).astype(jnp.float32)
    cells = station_cells.astype(jnp.float32)
    meta = jnp.concatenate(
        [
            flags,
            jnp.zeros((1, 64 - flags.shape[1]), jnp.float32),
            cells,
            jnp.zeros((1, 61), jnp.float32),
        ],
        axis=1,
    )
    f32 = jnp.float32
    plane = (n_space, nz)
    vmem = pl.BlockSpec(memory_space=pltpu.VMEM)
    anywhere = pl.BlockSpec(memory_space=pl.ANY)
    times, kernel_part = pl.pallas_call(
        functools.partial(kernel, dims),
        out_shape=(
            jax.ShapeDtypeStruct((ny, nz), f32),
            jax.ShapeDtypeStruct((own_rows, nz), f32),
        ),
        in_specs=[anywhere, vmem, vmem, vmem],
        out_specs=(anywhere, anywhere),
        scratch_shapes=[
            pltpu.VMEM((tall,) + plane, f32),
            pltpu.VMEM((tall,) + plane, f32),
            pltpu.VMEM((GROUP, n_space, 128), f32),
            pltpu.VMEM((GROUP, 1, events), f32),
            pltpu.VMEM((GROUP, tall + 2) + plane, f32),
            pltpu.VMEM((GROUP, tall + 2) + plane, f32),
            pltpu.VMEM((GROUP, tall + 2) + plane, f32),
            pltpu.VMEM((src_rows * n_space, nz), f32),
            pltpu.VMEM((GROUP, src_rows * n_space, nz), f32),
            pltpu.VMEM((2, GROUP, 3) + plane, f32),
            pltpu.VMEM((GROUP,) + plane, f32),
            pltpu.VMEM((6, src_rows - 2) + plane, f32),
            pltpu.VMEM((2, src_rows) + plane, f32),
            pltpu.VMEM((src_rows,) + plane, f32),
            pltpu.VMEM((rows + 2,) + plane, f32),
            pltpu.VMEM((rows,) + plane, f32),
            pltpu.VMEM((peers, rows, chunk_x, nz), f32),
            pltpu.VMEM((rows, chunk_x, nz), f32),
            pltpu.SemaphoreType.DMA((8,)),
            pltpu.SemaphoreType.DMA((8,)),
            pltpu.SemaphoreType.DMA((chunk_x,)),
        ],
        compiler_params=pltpu.CompilerParams(
            collective_id=0, has_side_effects=True, vmem_limit_bytes=48 << 20
        ),
    )(velocity[0], meta, event_cells, delays)
    return times[None, None], kernel_part[None]


def solution(mesh):
    n_src, n_space = mesh.shape["src"], mesh.shape["space"]

    def run(velocity, station_cells, event_cells, delays, active):
        dims = (n_src, n_space, velocity.shape[1], velocity.shape[2], event_cells.shape[1])
        return jax.shard_map(
            functools.partial(per_device, dims),
            mesh=mesh,
            in_specs=(
                P("space", None, None),
                P("src", None),
                P(),
                P("src", None),
                P(None, "src", "space", None),
            ),
            out_specs=(P("src", "space", None, None), P("space", "src", None)),
            check_vma=False,
        )(velocity, station_cells, event_cells, delays, active)

    return run
```

```python
import functools

import jax
import jax.numpy as jnp
from jax import lax
from jax.experimental import pallas as pl
from jax.experimental.pallas import tpu as pltpu
from jax.sharding import PartitionSpec as P

TY = 32
BIG = 1000000.0
HALO = 8
GROUP = 2
MESH = pl.DeviceIdType.MESH


def godunov(near_x, near_y, near_z, cost):
    low_xy = jnp.minimum(near_x, near_y)
    high_xy = jnp.maximum(near_x, near_y)
    lowest = jnp.minimum(low_xy, near_z)
    rest = jnp.maximum(low_xy, near_z)
    middle = jnp.minimum(high_xy, rest)
    highest = jnp.maximum(high_xy, rest)
    gap2 = middle - lowest
    gap3 = highest - lowest
    cost_sq = cost * cost
    gap2_sq = gap2 * gap2
    disc2 = 2.0 * cost_sq - gap2_sq
    reach = gap3 + gap3 - gap2
    two = disc2 <= reach * reach
    step = gap3 - gap2
    disc3 = 3.0 * cost_sq - (gap2_sq + gap3 * gap3 + step * step)
    disc = jnp.where(two, disc2, disc3)
    base = jnp.where(two, gap2, gap2 + gap3)
    scale = jnp.where(two, 0.5, 1.0 / 3.0)
    wide = lowest + (base + root(jnp.maximum(disc, 1e-30))) * scale
    return jnp.where(cost <= gap2, lowest + cost, wide)


def tiles_of(ref, index):
    return {
        (t, h): ref[index + (pl.ds(8 * t, 8), pl.ds(128 * h, 128))]
        for t in range(ref.shape[-2] // 8)
        for h in range(ref.shape[-1] // 128)
    }


def at_tile(t, h):
    return (pl.ds(8 * t, 8), pl.ds(128 * h, 128))


def beside_x(field, fill):
    sub = lax.broadcasted_iota(jnp.int32, (8, 128), 0)
    down = {key: pltpu.roll(value, 1, 0) for key, value in field.items()}
    up = {key: pltpu.roll(value, 7, 0) for key, value in field.items()}
    low = {(t, h): jnp.where(sub == 0, down.get((t - 1, h), fill), down[t, h]) for t, h in field}
    high = {(t, h): jnp.where(sub == 7, up.get((t + 1, h), fill), up[t, h]) for t, h in field}
    return low, high


def beside_z(field, fill):
    lane = lax.broadcasted_iota(jnp.int32, (8, 128), 1)
    down = {key: pltpu.roll(value, 1, 1) for key, value in field.items()}
    up = {key: pltpu.roll(value, 127, 1) for key, value in field.items()}
    low = {(t, h): jnp.where(lane == 0, down.get((t, h - 1), fill), down[t, h]) for t, h in field}
    high = {(t, h): jnp.where(lane == 127, up.get((t, h + 1), fill), up[t, h]) for t, h in field}
    return low, high


def root(value):
    return value * lax.rsqrt(jnp.maximum(value, 1e-30))


def kernel(
    dims,
    velocity_ref,
    meta_ref,
    events_hbm,
    delays_ref,
    times_out,
    kernel_out,
    events_ref,
    vel,
    slow,
    meta,
    delay,
    start,
    time_a,
    time_b,
    count,
    late,
    masks,
    spot,
    weights,
    source,
    adj_a,
    adj_b,
    dens,
    part,
    parts,
    total,
    local_sem,
    send_sem,
    recv_sem,
    last_sem,
):
    n_src, n_space, ny, nz, events = dims
    group = GROUP
    rows = ny // (n_space * group)
    peers = n_src // group
    chunk_x = n_space // peers
    own_rows = ny // n_src
    per_owner = own_rows // rows
    tall = rows + 2 * HALO
    s, p = lax.axis_index("src"), lax.axis_index("space")
    m, g = s // group, s % group
    block = g * n_space + p
    y_base = block * rows
    n_blocks = n_space * group

    def where_is(b):
        return (m * group + b // n_space, b % n_space)

    owner = block // per_owner
    targets = [(owner, chunk_x * m + k) for k in range(chunk_x)]
    sources = []
    for k in range(per_owner):
        b = s * per_owner + k
        sources.append(((p // chunk_x) * group + b // n_space, b % n_space))

    fetch_events = pltpu.make_async_copy(events_hbm, events_ref, local_sem)
    fetch_events.start()

    barrier = pltpu.get_barrier_semaphore()
    signals = 0
    for i in range(1, n_space):
        to = (s, (p + i) % n_space)
        pl.semaphore_signal(barrier, inc=1, device_id=to, device_id_type=MESH)
        signals += 1
    for dg in range(1, group):
        to = (m * group + (g + dg) % group, p)
        pl.semaphore_signal(barrier, inc=1, device_id=to, device_id_type=MESH)
        signals += 1
    for i in range(1, peers):
        to = (((m + i) % peers) * group + g, p)
        pl.semaphore_signal(barrier, inc=1, device_id=to, device_id_type=MESH)
        signals += 1
    for to in sources:
        mine = (to[0] == s) & (to[1] == p)

        @pl.when(jnp.logical_not(mine))
        def _():
            pl.semaphore_signal(barrier, inc=1, device_id=to, device_id_type=MESH)

        signals = signals + jnp.where(mine, 0, 1)
    pl.semaphore_wait(barrier, signals)

    own = pl.ds(HALO, rows)
    partners = [(m * group + (g + dg) % group, p) for dg in range(1, group)]
    for i in range(n_space):
        q = (p + i) % n_space
        line = meta.at[g, pl.ds(p, 1), :]
        if i == 0:
            pltpu.make_async_copy(meta_ref, line, recv_sem.at[1]).start()
        else:
            pltpu.make_async_remote_copy(
                meta_ref,
                line,
                send_sem.at[1],
                recv_sem.at[1],
                device_id=(s, q),
                device_id_type=MESH,
            ).start()
    for i in range(n_space):
        q = (p + i) % n_space
        piece = velocity_ref.at[pl.ds(pl.multiple_of((g * n_space + q) * rows, 8), rows), :]
        if i == 0:
            pltpu.make_async_copy(piece, vel.at[own, p, :], recv_sem.at[0]).start()
        else:
            pltpu.make_async_remote_copy(
                piece,
                vel.at[own, p, :],
                send_sem.at[0],
                recv_sem.at[0],
                device_id=(s, q),
                device_id_type=MESH,
            ).start()
    pltpu.make_async_copy(delays_ref, delay.at[g], recv_sem.at[2]).start()
    for to in partners:
        pltpu.make_async_remote_copy(
            delays_ref,
            delay.at[g],
            send_sem.at[2],
            recv_sem.at[2],
            device_id=to,
            device_id_type=MESH,
        ).start()

    src_rows = rows + 10
    cells = src_rows * n_space
    step_events = 1024
    steps = events // step_events
    count[...] = jnp.zeros_like(count)
    late[...] = jnp.zeros_like(late)
    fetch_events.wait()
    pltpu.make_async_copy(delay, delay, recv_sem.at[2]).wait()

    def add_events(c, carry):
        at = pl.ds(pl.multiple_of(c * step_events, step_events), step_events)
        event_x = events_ref[0:1, at]
        event_y = events_ref[1:2, at]
        event_z = events_ref[2:3, at]
        key = (event_y - (y_base - 5)) * n_space + event_x
        cell = lax.broadcasted_iota(jnp.int32, (cells, step_events), 0)
        left = jnp.where(cell == key, 1.0, 0.0).astype(jnp.bfloat16)
        deep = lax.broadcasted_iota(jnp.int32, (nz, step_events), 0) == event_z
        contract = (((1,), (1,)), ((), ()))

        def product(value):
            right = jnp.where(deep, value, 0.0).astype(jnp.bfloat16)
            return lax.dot_general(left, right, contract, preferred_element_type=jnp.float32)

        count[...] += product(1.0)
        for k in range(group):
            lateness = delay[k, 0:1, at]
            coarse = lateness.astype(jnp.bfloat16).astype(jnp.float32)
            late[k] += product(coarse) + product(lateness - coarse)
        return carry

    cut_a, cut_b = (steps * 3) // 8, (steps * 5) // 8
    lax.fori_loop(0, cut_a, add_events, 0)

    pltpu.make_async_copy(meta.at[g], meta.at[g], recv_sem.at[1]).wait()
    for to in partners:
        pltpu.make_async_remote_copy(
            meta.at[g],
            meta.at[g],
            send_sem.at[3],
            recv_sem.at[3],
            device_id=to,
            device_id_type=MESH,
        ).start()
    lax.fori_loop(cut_a, cut_b, add_events, 0)

    pltpu.make_async_copy(vel.at[own], vel.at[own], recv_sem.at[0]).wait()
    for dg in range(1, group):
        other = (g + dg) % group
        pltpu.make_async_copy(meta.at[other], meta.at[other], recv_sem.at[3]).wait()
    before = where_is((block + n_blocks - 1) % n_blocks)
    after = where_is((block + 1) % n_blocks)
    to_before = pltpu.make_async_remote_copy(
        vel.at[pl.ds(HALO, HALO)],
        vel.at[pl.ds(HALO + rows, HALO)],
        send_sem.at[4],
        recv_sem.at[4],
        device_id=before,
        device_id_type=MESH,
    )
    to_after = pltpu.make_async_remote_copy(
        vel.at[pl.ds(rows, HALO)],
        vel.at[pl.ds(0, HALO)],
        send_sem.at[5],
        recv_sem.at[5],
        device_id=after,
        device_id_type=MESH,
    )
    to_before.start()
    to_after.start()
    lax.fori_loop(cut_b, steps, add_events, 0)

    lane = lax.broadcasted_iota(jnp.int32, (n_space, 128), 1)
    layer_f = lax.broadcasted_iota(jnp.int32, (n_space, nz), 0).astype(jnp.float32)
    depth_f = lax.broadcasted_iota(jnp.int32, (n_space, nz), 1).astype(jnp.float32)
    first_tile = (y_base - HALO + TY) // TY - 1
    tile_count = ny // TY

    def column(k, index):
        picked = jnp.where(lane == index, meta[k], 0.0)
        return jnp.broadcast_to(jnp.sum(picked, axis=1, keepdims=True), (n_space, nz))

    def row_valid(y):
        return (y >= 0) & (y < ny)

    for k in range(group):
        for r in range(2):
            for t in range(2):
                masks[r, k, t] = column(k, r * tile_count + first_tile + t)
            masks[r, k, 2] = jnp.zeros((n_space, nz), jnp.float32)
        cell_x, cell_y, cell_z = column(k, 64), column(k, 65), column(k, 66)
        here = (layer_f == cell_x) & (depth_f == cell_z)
        spot[k] = jnp.where(here, cell_y, -1.0)
        flat = (layer_f - cell_x) * (layer_f - cell_x) + (depth_f - cell_z) * (depth_f - cell_z)

        def init_row(j, carry):
            y = y_base - HALO - 1 + j
            diff = y.astype(jnp.float32) - cell_y
            start[k, j] = jnp.where(row_valid(y), root(flat + diff * diff), BIG)
            return carry

        lax.fori_loop(0, tall + 2, init_row, 0, unroll=2)

    to_before.wait_recv()
    to_after.wait_recv()

    def slow_row(j, carry):
        slow[j] = 1.0 / vel[j]
        return carry

    lax.fori_loop(0, tall, slow_row, 0, unroll=4)

    def sweep(old, new, low, high, r):
        def row(j, carry):
            y = y_base - HALO + j
            kind = jnp.where(row_valid(y), (y + TY) // TY - 1 - first_tile, 2)
            for k in range(group):
                centre = tiles_of(old, (k, j + 1))
                x_low, x_high = beside_x(centre, BIG)
                z_low, z_high = beside_z(centre, BIG)
                for t, h in centre:
                    tile = at_tile(t, h)
                    update = godunov(
                        jnp.minimum(x_low[t, h], x_high[t, h]),
                        jnp.minimum(old[(k, j) + tile], old[(k, j + 2) + tile]),
                        jnp.minimum(z_low[t, h], z_high[t, h]),
                        slow[(j,) + tile],
                    )
                    chosen = (masks[(r, k, kind) + tile] > 0.0) & (
                        spot[(k,) + tile] != y.astype(jnp.float32)
                    )
                    new[(k, j + 1) + tile] = jnp.where(chosen, update, centre[t, h])
            return carry

        lax.fori_loop(low, high, row, 0, unroll=4)

    inner = pl.ds(HALO + 1, rows)
    sweep(start, time_a, 0, tall, 0)
    sweep(time_a, time_b, 1, tall - 1, 0)
    sweep(time_b, time_a, 2, tall - 2, 1)
    sweep(time_a, time_b, 3, tall - 3, 1)
    for k in range(group):
        for i in range(n_space):
            q = (p + i) % n_space
            piece = time_b.at[k, inner, q, :]
            place = times_out.at[pl.ds(pl.multiple_of(y_base, 8), rows), :]
            to_src = m * group + k

            def send(piece=piece, place=place, to_src=to_src, q=q):
                pltpu.make_async_remote_copy(
                    piece,
                    place,
                    send_sem.at[6],
                    recv_sem.at[6],
                    device_id=(to_src, q),
                    device_id_type=MESH,
                ).start()

            if i:
                send()
            else:

                @pl.when(g == k)
                def _():
                    pltpu.make_async_copy(piece, place, recv_sem.at[6]).start()

                @pl.when(g != k)
                def _():
                    send()

    def source_row(i, carry):
        at = pl.ds(pl.multiple_of(i * n_space, n_space), n_space)
        for k in range(group):
            shift = time_b[k, i + 4] - start[k, i + 4]
            source[k, i] = count[at, :] * shift - late[k, at, :]
        return carry

    lax.fori_loop(0, src_rows, source_row, 0, unroll=2)

    def weight_row(i, carry):
        j = i + 5
        for k in range(group):
            centre = tiles_of(time_b, (k, j))
            x_low, x_high = beside_x(centre, 0.0)
            z_low, z_high = beside_z(centre, 0.0)
            for t, h in centre:
                tile = at_tile(t, h)
                rate = vel[(i + 4,) + tile] * (1.0 / 6.0)
                around = (
                    x_low[t, h],
                    x_high[t, h],
                    time_b[(k, j - 1) + tile],
                    time_b[(k, j + 1) + tile],
                    z_low[t, h],
                    z_high[t, h],
                )
                for d, near in enumerate(around):
                    weights[(k, d, i) + tile] = jnp.maximum(near - centre[t, h], 0.0) * rate
        return carry

    lax.fori_loop(0, src_rows - 2, weight_row, 0, unroll=4)

    def adjoint_sweep(old, new, low, high):
        def row(i, carry):
            for k in range(group):
                centre = tiles_of(old, (k, i))
                x_low, x_high = beside_x(centre, 0.0)
                z_low, z_high = beside_z(centre, 0.0)
                for t, h in centre:
                    tile = at_tile(t, h)
                    weight = [weights[(k, d, i - 1) + tile] for d in range(6)]
                    along_x = weight[0] * x_low[t, h] + weight[1] * x_high[t, h]
                    along_y = weight[2] * old[(k, i - 1) + tile] + weight[3] * old[(k, i + 1) + tile]
                    along_z = weight[4] * z_low[t, h] + weight[5] * z_high[t, h]
                    new[(k, i) + tile] = source[(k, i) + tile] + along_x + (along_y + along_z)
            return carry

        lax.fori_loop(low, high, row, 0, unroll=4)

    adjoint_sweep(source, adj_a, 1, src_rows - 1)
    adjoint_sweep(adj_a, adj_b, 2, src_rows - 2)
    adjoint_sweep(adj_b, adj_a, 3, src_rows - 3)
    adjoint_sweep(adj_a, adj_b, 4, src_rows - 4)

    def density_row(i, carry):
        value = adj_b[0, i + 4]
        for k in range(1, group):
            value = value + adj_b[k, i + 4]
        dens[i] = slow[i + HALO - 1] * value
        return carry

    lax.fori_loop(0, rows + 2, density_row, 0, unroll=2)

    def smooth_row(i, carry):
        first, middle, last = (tiles_of(dens, (i + d,)) for d in range(3))
        value = {key: first[key] + 2.0 * middle[key] + last[key] for key in first}
        for beside in (beside_x, beside_z):
            low, high = beside(value, 0.0)
            value = {key: low[key] + 2.0 * value[key] + high[key] for key in value}
        for t, h in value:
            part[(i,) + at_tile(t, h)] = value[t, h] * (1.0 / 64.0)
        return carry

    lax.fori_loop(0, rows, smooth_row, 0, unroll=2)

    for i in range(peers):
        q = (m + i) % peers
        piece = part.at[:, pl.ds(pl.multiple_of(q * chunk_x, chunk_x), chunk_x), :]
        if i == 0:
            pltpu.make_async_copy(piece, parts.at[m], recv_sem.at[7]).start()
        else:
            pltpu.make_async_remote_copy(
                piece,
                parts.at[m],
                send_sem.at[7],
                recv_sem.at[7],
                device_id=(q * group + g, p),
                device_id_type=MESH,
            ).start()
    pltpu.make_async_copy(parts, parts, recv_sem.at[7]).wait()
    summed = parts[0]
    for i in range(1, peers):
        summed = summed + parts[i]
    total[...] = summed
    place_k = block % per_owner
    for k in range(chunk_x):
        to = targets[k]
        piece = total.at[:, k, :]
        place = kernel_out.at[pl.ds(pl.multiple_of(place_k * rows, 8), rows), :]
        mine = (to[0] == s) & (to[1] == p)

        @pl.when(mine)
        def _():
            pltpu.make_async_copy(piece, place, recv_sem.at[8]).start()

        @pl.when(jnp.logical_not(mine))
        def _():
            pltpu.make_async_remote_copy(
                piece,
                place,
                last_sem.at[k],
                recv_sem.at[8],
                device_id=to,
                device_id_type=MESH,
            ).start()

    def drain(ref, sem):
        pltpu.make_async_copy(ref, ref, sem).wait()

    drain(velocity_ref.at[pl.ds(0, (n_space - 1) * rows), :], send_sem.at[0])
    drain(meta.at[0, pl.ds(0, n_space - 8), :], send_sem.at[1])
    for _ in range(7):
        drain(meta_ref, send_sem.at[1])
    for _ in partners:
        drain(delay.at[0], send_sem.at[2])
        drain(meta.at[0], send_sem.at[3])
    to_before.wait_send()
    to_after.wait_send()
    drain(times_out.at[pl.ds(0, (n_blocks - 1) * rows), :], send_sem.at[6])
    drain(parts.at[pl.ds(1, peers - 1)], send_sem.at[7])
    for k in range(chunk_x):
        to = targets[k]
        mine = (to[0] == s) & (to[1] == p)

        @pl.when(jnp.logical_not(mine))
        def _():
            drain(total.at[:, k, :], last_sem.at[k])

    drain(times_out, recv_sem.at[6])
    drain(kernel_out, recv_sem.at[8])


def per_device(dims, velocity, station_cells, event_cells, delays, active):
    n_src, n_space, ny, nz, events = dims
    rows = ny // (n_space * GROUP)
    tall = rows + 2 * HALO
    peers = n_src // GROUP
    chunk_x = n_space // peers
    own_rows = ny // n_src
    src_rows = rows + 10
    flags = active.reshape(1, -1).astype(jnp.float32)
    cells = station_cells.astype(jnp.float32)
    meta = jnp.concatenate(
        [
            flags,
            jnp.zeros((1, 64 - flags.shape[1]), jnp.float32),
            cells,
            jnp.zeros((1, 61), jnp.float32),
        ],
        axis=1,
    )
    f32 = jnp.float32
    plane = (n_space, nz)
    vmem = pl.BlockSpec(memory_space=pltpu.VMEM)
    anywhere = pl.BlockSpec(memory_space=pl.ANY)
    hbm = pl.BlockSpec(memory_space=pltpu.HBM)
    times, kernel_part = pl.pallas_call(
        functools.partial(kernel, dims),
        out_shape=(
            jax.ShapeDtypeStruct((ny, nz), f32),
            jax.ShapeDtypeStruct((own_rows, nz), f32),
        ),
        in_specs=[hbm, vmem, hbm, hbm],
        out_specs=(anywhere, anywhere),
        scratch_shapes=[
            pltpu.VMEM((3, events), jnp.int32),
            pltpu.VMEM((tall,) + plane, f32),
            pltpu.VMEM((tall,) + plane, f32),
            pltpu.VMEM((GROUP, n_space, 128), f32),
            pltpu.VMEM((GROUP, 1, events), f32),
            pltpu.VMEM((GROUP, tall + 2) + plane, f32),
            pltpu.VMEM((GROUP, tall + 2) + plane, f32),
            pltpu.VMEM((GROUP, tall + 2) + plane, f32),
            pltpu.VMEM((src_rows * n_space, nz), f32),
            pltpu.VMEM((GROUP, src_rows * n_space, nz), f32),
            pltpu.VMEM((2, GROUP, 3) + plane, f32),
            pltpu.VMEM((GROUP,) + plane, f32),
            pltpu.VMEM((GROUP, 6, src_rows - 2) + plane, f32),
            pltpu.VMEM((GROUP, src_rows) + plane, f32),
            pltpu.VMEM((GROUP, src_rows) + plane, f32),
            pltpu.VMEM((GROUP, src_rows) + plane, f32),
            pltpu.VMEM((rows + 2,) + plane, f32),
            pltpu.VMEM((rows,) + plane, f32),
            pltpu.VMEM((peers, rows, chunk_x, nz), f32),
            pltpu.VMEM((rows, chunk_x, nz), f32),
            pltpu.SemaphoreType.DMA,
            pltpu.SemaphoreType.DMA((8,)),
            pltpu.SemaphoreType.DMA((9,)),
            pltpu.SemaphoreType.DMA((chunk_x,)),
        ],
        compiler_params=pltpu.CompilerParams(
            collective_id=0, has_side_effects=True, vmem_limit_bytes=60 << 20
        ),
    )(velocity[0], meta, event_cells, delays)
    return times[None, None], kernel_part[None]


def solution(mesh):
    n_src, n_space = mesh.shape["src"], mesh.shape["space"]

    def run(velocity, station_cells, event_cells, delays, active):
        dims = (n_src, n_space, velocity.shape[1], velocity.shape[2], event_cells.shape[1])
        return jax.shard_map(
            functools.partial(per_device, dims),
            mesh=mesh,
            in_specs=(
                P("space", None, None),
                P("src", None),
                P(),
                P("src", None),
                P(None, "src", "space", None),
            ),
            out_specs=(P("src", "space", None, None), P("space", "src", None)),
            check_vma=False,
        )(velocity, station_cells, event_cells, delays, active)

    return run
```

```python
import functools

import jax
import jax.numpy as jnp
from jax import lax
from jax.experimental import pallas as pl
from jax.experimental.pallas import tpu as pltpu
from jax.sharding import PartitionSpec as P

TY = 32
BIG = 1000000.0
HALO = 8
GROUP = 2
MESH = pl.DeviceIdType.MESH


def godunov(near_x, near_y, near_z, cost):
    low_xy = jnp.minimum(near_x, near_y)
    high_xy = jnp.maximum(near_x, near_y)
    lowest = jnp.minimum(low_xy, near_z)
    rest = jnp.maximum(low_xy, near_z)
    middle = jnp.minimum(high_xy, rest)
    highest = jnp.maximum(high_xy, rest)
    gap2 = middle - lowest
    gap3 = highest - lowest
    cost_sq = cost * cost
    gap2_sq = gap2 * gap2
    disc2 = 2.0 * cost_sq - gap2_sq
    reach = gap3 + gap3 - gap2
    two = disc2 <= reach * reach
    step = gap3 - gap2
    disc3 = 3.0 * cost_sq - (gap2_sq + gap3 * gap3 + step * step)
    disc = jnp.where(two, disc2, disc3)
    base = jnp.where(two, gap2, gap2 + gap3)
    scale = jnp.where(two, 0.5, 1.0 / 3.0)
    wide = lowest + (base + root(jnp.maximum(disc, 1e-30))) * scale
    return jnp.where(cost <= gap2, lowest + cost, wide)


def tiles_of(ref, index):
    return {
        (t, h): ref[index + (pl.ds(8 * t, 8), pl.ds(128 * h, 128))]
        for t in range(ref.shape[-2] // 8)
        for h in range(ref.shape[-1] // 128)
    }


def at_tile(t, h):
    return (pl.ds(8 * t, 8), pl.ds(128 * h, 128))


def beside_x(field, fill):
    sub = lax.broadcasted_iota(jnp.int32, (8, 128), 0)
    down = {key: pltpu.roll(value, 1, 0) for key, value in field.items()}
    up = {key: pltpu.roll(value, 7, 0) for key, value in field.items()}
    low = {(t, h): jnp.where(sub == 0, down.get((t - 1, h), fill), down[t, h]) for t, h in field}
    high = {(t, h): jnp.where(sub == 7, up.get((t + 1, h), fill), up[t, h]) for t, h in field}
    return low, high


def beside_z(field, fill):
    lane = lax.broadcasted_iota(jnp.int32, (8, 128), 1)
    down = {key: pltpu.roll(value, 1, 1) for key, value in field.items()}
    up = {key: pltpu.roll(value, 127, 1) for key, value in field.items()}
    low = {(t, h): jnp.where(lane == 0, down.get((t, h - 1), fill), down[t, h]) for t, h in field}
    high = {(t, h): jnp.where(lane == 127, up.get((t, h + 1), fill), up[t, h]) for t, h in field}
    return low, high


def root(value):
    return value * lax.rsqrt(jnp.maximum(value, 1e-30))


def kernel(
    dims,
    velocity_ref,
    cells_ref,
    flags_ref,
    events_hbm,
    delays_ref,
    times_out,
    kernel_out,
    meta_ref,
    events_ref,
    vel,
    slow,
    meta,
    delay,
    start,
    time_a,
    time_b,
    landed,
    masks,
    spot,
    weights,
    source,
    adj_a,
    adj_b,
    dens,
    part,
    parts,
    total,
    local_sem,
    send_sem,
    recv_sem,
    halo_send,
    halo_recv,
    last_sem,
):
    n_src, n_space, ny, nz, events = dims
    group = GROUP
    rows = ny // (n_space * group)
    peers = n_src // group
    chunk_x = n_space // peers
    own_rows = ny // n_src
    per_owner = own_rows // rows
    tall = rows + 2 * HALO
    s, p = lax.axis_index("src"), lax.axis_index("space")
    m, g = s // group, s % group
    block = g * n_space + p
    y_base = block * rows
    n_blocks = n_space * group

    def where_is(b):
        return (m * group + b // n_space, b % n_space)

    owner = block // per_owner
    targets = [(owner, chunk_x * m + k) for k in range(chunk_x)]
    sources = []
    for k in range(per_owner):
        b = s * per_owner + k
        sources.append(((p // chunk_x) * group + b // n_space, b % n_space))

    fetch_events = pltpu.make_async_copy(events_hbm, events_ref, local_sem)
    fetch_events.start()

    lane = lax.broadcasted_iota(jnp.int32, (1, 128), 1)
    line = jnp.zeros((1, 128), jnp.float32)
    tile_count = ny // TY
    for r in range(2):
        for t in range(tile_count):
            flag = flags_ref[r, t].astype(jnp.float32)
            line = jnp.where(lane == r * tile_count + t, flag, line)
    for d in range(3):
        line = jnp.where(lane == 64 + d, cells_ref[0, d].astype(jnp.float32), line)
    meta_ref[...] = line

    barrier = pltpu.get_barrier_semaphore()
    signals = 0
    for i in range(1, n_space):
        to = (s, (p + i) % n_space)
        pl.semaphore_signal(barrier, inc=1, device_id=to, device_id_type=MESH)
        signals += 1
    for dg in range(1, group):
        to = (m * group + (g + dg) % group, p)
        pl.semaphore_signal(barrier, inc=1, device_id=to, device_id_type=MESH)
        signals += 1
    for i in range(1, peers):
        to = (((m + i) % peers) * group + g, p)
        pl.semaphore_signal(barrier, inc=1, device_id=to, device_id_type=MESH)
        signals += 1
    for to in sources:
        mine = (to[0] == s) & (to[1] == p)

        @pl.when(jnp.logical_not(mine))
        def _():
            pl.semaphore_signal(barrier, inc=1, device_id=to, device_id_type=MESH)

        signals = signals + jnp.where(mine, 0, 1)
    pl.semaphore_wait(barrier, signals)

    own = pl.ds(HALO, rows)
    partners = [(m * group + (g + dg) % group, p) for dg in range(1, group)]
    for i in range(n_space):
        q = (p + i) % n_space
        line = meta.at[g, pl.ds(p, 1), :]
        if i == 0:
            pltpu.make_async_copy(meta_ref, line, recv_sem.at[1]).start()
        else:
            pltpu.make_async_remote_copy(
                meta_ref,
                line,
                send_sem.at[1],
                recv_sem.at[1],
                device_id=(s, q),
                device_id_type=MESH,
            ).start()
    half = n_space // 2
    near_half = (p // half) * half
    far_half = half - near_half
    for i in range(n_space):
        if i < half:
            q = near_half + (p + i) % half
        else:
            q = far_half + (p + i) % half
        piece = velocity_ref.at[pl.ds(pl.multiple_of((g * n_space + q) * rows, 8), rows), :]
        arrived = recv_sem.at[0] if i < half else recv_sem.at[9]
        if i == 0:
            pltpu.make_async_copy(piece, vel.at[own, p, :], arrived).start()
        else:
            pltpu.make_async_remote_copy(
                piece,
                vel.at[own, p, :],
                send_sem.at[0],
                arrived,
                device_id=(s, q),
                device_id_type=MESH,
            ).start()
    pltpu.make_async_copy(delays_ref, delay.at[g], recv_sem.at[2]).start()
    for to in partners:
        pltpu.make_async_remote_copy(
            delays_ref,
            delay.at[g],
            send_sem.at[2],
            recv_sem.at[2],
            device_id=to,
            device_id_type=MESH,
        ).start()

    src_rows = rows + 10
    cells = rows * n_space
    step_events = 1024
    steps = events // step_events
    mine_rows = pl.ds(5, rows)
    landed[mine_rows] = jnp.zeros((rows, 1 + group, n_space, nz), jnp.float32)
    fetch_events.wait()
    pltpu.make_async_copy(delay, delay, recv_sem.at[2]).wait()

    def add_events(c, carry):
        at = pl.ds(pl.multiple_of(c * step_events, step_events), step_events)
        event_x = events_ref[0:1, at]
        event_y = events_ref[1:2, at]
        event_z = events_ref[2:3, at]
        key = (event_y - y_base) * n_space + event_x
        cell = lax.broadcasted_iota(jnp.int32, (cells, step_events), 0)
        left = jnp.where(cell == key, 1.0, 0.0).astype(jnp.bfloat16)
        deep = lax.broadcasted_iota(jnp.int32, (nz, step_events), 0) == event_z
        contract = (((1,), (1,)), ((), ()))

        def product(value):
            right = jnp.where(deep, value, 0.0).astype(jnp.bfloat16)
            out = lax.dot_general(left, right, contract, preferred_element_type=jnp.float32)
            return out.reshape(rows, n_space, nz)

        landed[mine_rows, 0] += product(1.0)
        for k in range(group):
            lateness = delay[k, 0:1, at]
            coarse = lateness.astype(jnp.bfloat16).astype(jnp.float32)
            landed[mine_rows, 1 + k] += product(coarse) + product(lateness - coarse)
        return carry

    wide_lane = lax.broadcasted_iota(jnp.int32, (n_space, 128), 1)
    layer_f = lax.broadcasted_iota(jnp.int32, (n_space, nz), 0).astype(jnp.float32)
    depth_f = lax.broadcasted_iota(jnp.int32, (n_space, nz), 1).astype(jnp.float32)
    first_tile = (y_base - HALO + TY) // TY - 1

    def column(k, index):
        picked = jnp.where(wide_lane == index, meta[k], 0.0)
        return jnp.broadcast_to(jnp.sum(picked, axis=1, keepdims=True), (n_space, nz))

    def row_valid(y):
        return (y >= 0) & (y < ny)

    def init_fields():
        for dg in range(1, group):
            other = (g + dg) % group
            pltpu.make_async_copy(meta.at[other], meta.at[other], recv_sem.at[3]).wait()
        for k in range(group):
            for r in range(2):
                for t in range(2):
                    masks[r, k, t] = column(k, r * tile_count + first_tile + t)
                masks[r, k, 2] = jnp.zeros((n_space, nz), jnp.float32)
            cell_x, cell_y, cell_z = column(k, 64), column(k, 65), column(k, 66)
            here = (layer_f == cell_x) & (depth_f == cell_z)
            spot[k] = jnp.where(here, cell_y, -1.0)
            off_x, off_z = layer_f - cell_x, depth_f - cell_z
            flat = off_x * off_x + off_z * off_z

            def init_row(j, carry):
                y = y_base - HALO - 1 + j
                diff = y.astype(jnp.float32) - cell_y
                start[k, j] = jnp.where(row_valid(y), root(flat + diff * diff), BIG)
                return carry

            lax.fori_loop(0, tall + 2, init_row, 0, unroll=2)

    before = where_is((block + n_blocks - 1) % n_blocks)
    after = where_is((block + 1) % n_blocks)
    cut = steps // 2
    lax.fori_loop(0, cut, add_events, 0)

    pltpu.make_async_copy(meta.at[g], meta.at[g], recv_sem.at[1]).wait()
    for to in partners:
        pltpu.make_async_remote_copy(
            meta.at[g],
            meta.at[g],
            send_sem.at[3],
            recv_sem.at[3],
            device_id=to,
            device_id_type=MESH,
        ).start()
    lax.fori_loop(cut, steps, add_events, 0)

    halos = []
    for n, (x_at, arrived) in enumerate(((near_half, 0), (far_half, 9))):
        layers = pl.ds(pl.multiple_of(x_at, half), half)
        here = vel.at[own, layers, :]
        pltpu.make_async_copy(here, here, recv_sem.at[arrived]).wait()
        for d, (at, there, to) in enumerate(
            ((HALO, HALO + rows, before), (rows, 0, after))
        ):
            halo = pltpu.make_async_remote_copy(
                vel.at[pl.ds(at, HALO), layers, :],
                vel.at[pl.ds(there, HALO), layers, :],
                halo_send.at[2 * n + d],
                halo_recv.at[2 * n + d],
                device_id=to,
                device_id_type=MESH,
            )
            halo.start()
            halos.append(halo)
        if n == 0:
            init_fields()

    events_before = pltpu.make_async_remote_copy(
        landed.at[pl.ds(5, 5)],
        landed.at[pl.ds(5 + rows, 5)],
        send_sem.at[4],
        recv_sem.at[4],
        device_id=before,
        device_id_type=MESH,
    )
    events_after = pltpu.make_async_remote_copy(
        landed.at[pl.ds(rows, 5)],
        landed.at[pl.ds(0, 5)],
        send_sem.at[5],
        recv_sem.at[5],
        device_id=after,
        device_id_type=MESH,
    )

    def slow_row(j, carry):
        slow[j] = 1.0 / vel[j]
        return carry

    def sweep_row(old, new, r, j):
        y = y_base - HALO + j
        kind = jnp.where(row_valid(y), (y + TY) // TY - 1 - first_tile, 2)
        for k in range(group):
            centre = tiles_of(old, (k, j + 1))
            x_low, x_high = beside_x(centre, BIG)
            z_low, z_high = beside_z(centre, BIG)
            for t, h in centre:
                tile = at_tile(t, h)
                update = godunov(
                    jnp.minimum(x_low[t, h], x_high[t, h]),
                    jnp.minimum(old[(k, j) + tile], old[(k, j + 2) + tile]),
                    jnp.minimum(z_low[t, h], z_high[t, h]),
                    slow[(j,) + tile],
                )
                chosen = (masks[(r, k, kind) + tile] > 0.0) & (
                    spot[(k,) + tile] != y.astype(jnp.float32)
                )
                new[(k, j + 1) + tile] = jnp.where(chosen, update, centre[t, h])

    stages = ((start, time_a, 0), (time_a, time_b, 0), (time_b, time_a, 1), (time_a, time_b, 1))
    lax.fori_loop(HALO, HALO + rows, slow_row, 0, unroll=4)
    for n, (old, new, r) in enumerate(stages):

        def inside(j, carry):
            sweep_row(old, new, r, j)
            return carry

        lax.fori_loop(HALO + n, HALO + rows - n, inside, 0, unroll=2)

    for halo in halos:
        halo.wait_recv()
    events_before.start()
    events_after.start()
    lax.fori_loop(0, HALO, slow_row, 0, unroll=4)
    lax.fori_loop(HALO + rows, tall, slow_row, 0, unroll=4)
    for n, (old, new, r) in enumerate(stages):

        def outside(i, carry):
            sweep_row(old, new, r, n + i)
            sweep_row(old, new, r, HALO + rows - n + i)
            return carry

        lax.fori_loop(0, HALO, outside, 0, unroll=2)

    inner = pl.ds(HALO + 1, rows)

    def send_times(k):
        for i in range(n_space):
            q = (p + i) % n_space
            piece = time_b.at[k, inner, q, :]
            place = times_out.at[pl.ds(pl.multiple_of(y_base, 8), rows), :]
            to_src = m * group + k

            def send(piece=piece, place=place, to_src=to_src, q=q):
                pltpu.make_async_remote_copy(
                    piece,
                    place,
                    send_sem.at[6],
                    recv_sem.at[6],
                    device_id=(to_src, q),
                    device_id_type=MESH,
                ).start()

            if i:
                send()
            else:

                @pl.when(g == k)
                def _():
                    pltpu.make_async_copy(piece, place, recv_sem.at[6]).start()

                @pl.when(g != k)
                def _():
                    send()

    send_times(0)

    def weight_row(i, carry):
        j = i + 5
        for k in range(group):
            centre = tiles_of(time_b, (k, j))
            x_low, x_high = beside_x(centre, 0.0)
            z_low, z_high = beside_z(centre, 0.0)
            for t, h in centre:
                tile = at_tile(t, h)
                rate = vel[(i + 4,) + tile] * (1.0 / 6.0)
                around = (
                    x_low[t, h],
                    x_high[t, h],
                    time_b[(k, j - 1) + tile],
                    time_b[(k, j + 1) + tile],
                    z_low[t, h],
                    z_high[t, h],
                )
                for d, near in enumerate(around):
                    weights[(k, d, i) + tile] = jnp.maximum(near - centre[t, h], 0.0) * rate
        return carry

    lax.fori_loop(0, src_rows - 2, weight_row, 0, unroll=4)

    events_before.wait_recv()
    events_after.wait_recv()

    def source_row(i, carry):
        valid = row_valid(y_base - 5 + i)
        for k in range(group):
            shift = time_b[k, i + 4] - start[k, i + 4]
            value = landed[i, 0] * shift - landed[i, 1 + k]
            source[k, i] = jnp.where(valid, value, 0.0)
        return carry

    lax.fori_loop(0, src_rows, source_row, 0, unroll=2)

    def adjoint_sweep(old, new, low, high):
        def row(i, carry):
            for k in range(group):
                centre = tiles_of(old, (k, i))
                x_low, x_high = beside_x(centre, 0.0)
                z_low, z_high = beside_z(centre, 0.0)
                for t, h in centre:
                    tile = at_tile(t, h)
                    weight = [weights[(k, d, i - 1) + tile] for d in range(6)]
                    along_x = weight[0] * x_low[t, h] + weight[1] * x_high[t, h]
                    along_y = weight[2] * old[(k, i - 1) + tile] + weight[3] * old[(k, i + 1) + tile]
                    along_z = weight[4] * z_low[t, h] + weight[5] * z_high[t, h]
                    new[(k, i) + tile] = source[(k, i) + tile] + along_x + (along_y + along_z)
            return carry

        lax.fori_loop(low, high, row, 0, unroll=4)

    adjoint_sweep(source, adj_a, 1, src_rows - 1)
    adjoint_sweep(adj_a, adj_b, 2, src_rows - 2)
    adjoint_sweep(adj_b, adj_a, 3, src_rows - 3)
    adjoint_sweep(adj_a, adj_b, 4, src_rows - 4)

    def density_row(i, carry):
        value = adj_b[0, i + 4]
        for k in range(1, group):
            value = value + adj_b[k, i + 4]
        dens[i] = slow[i + HALO - 1] * value
        return carry

    lax.fori_loop(0, rows + 2, density_row, 0, unroll=2)

    def smooth_row(i, carry):
        first, middle, last = (tiles_of(dens, (i + d,)) for d in range(3))
        value = {key: first[key] + 2.0 * middle[key] + last[key] for key in first}
        for beside in (beside_x, beside_z):
            low, high = beside(value, 0.0)
            value = {key: low[key] + 2.0 * value[key] + high[key] for key in value}
        for t, h in value:
            part[(i,) + at_tile(t, h)] = value[t, h] * (1.0 / 64.0)
        return carry

    lax.fori_loop(0, rows, smooth_row, 0, unroll=2)

    for i in range(peers):
        q = (m + i) % peers
        piece = part.at[:, pl.ds(pl.multiple_of(q * chunk_x, chunk_x), chunk_x), :]
        if i == 0:
            pltpu.make_async_copy(piece, parts.at[m], recv_sem.at[7]).start()
        else:
            pltpu.make_async_remote_copy(
                piece,
                parts.at[m],
                send_sem.at[7],
                recv_sem.at[7],
                device_id=(q * group + g, p),
                device_id_type=MESH,
            ).start()
    for k in range(1, group):
        send_times(k)
    pltpu.make_async_copy(parts, parts, recv_sem.at[7]).wait()
    summed = parts[0]
    for i in range(1, peers):
        summed = summed + parts[i]
    total[...] = summed
    place_k = block % per_owner
    for k in range(chunk_x):
        to = targets[k]
        piece = total.at[:, k, :]
        place = kernel_out.at[pl.ds(pl.multiple_of(place_k * rows, 8), rows), :]
        mine = (to[0] == s) & (to[1] == p)

        @pl.when(mine)
        def _():
            pltpu.make_async_copy(piece, place, recv_sem.at[8]).start()

        @pl.when(jnp.logical_not(mine))
        def _():
            pltpu.make_async_remote_copy(
                piece,
                place,
                last_sem.at[k],
                recv_sem.at[8],
                device_id=to,
                device_id_type=MESH,
            ).start()

    def drain(ref, sem):
        pltpu.make_async_copy(ref, ref, sem).wait()

    drain(velocity_ref.at[pl.ds(0, (n_space - 1) * rows), :], send_sem.at[0])
    drain(meta.at[0, pl.ds(0, n_space - 8), :], send_sem.at[1])
    for _ in range(7):
        drain(meta_ref, send_sem.at[1])
    for _ in partners:
        drain(delay.at[0], send_sem.at[2])
        drain(meta.at[0], send_sem.at[3])
    for halo in halos:
        halo.wait_send()
    events_before.wait_send()
    events_after.wait_send()
    drain(times_out.at[pl.ds(0, (n_blocks - 1) * rows), :], send_sem.at[6])
    drain(parts.at[pl.ds(1, peers - 1)], send_sem.at[7])
    for k in range(chunk_x):
        to = targets[k]
        mine = (to[0] == s) & (to[1] == p)

        @pl.when(jnp.logical_not(mine))
        def _():
            drain(total.at[:, k, :], last_sem.at[k])

    drain(times_out, recv_sem.at[6])
    drain(kernel_out, recv_sem.at[8])


def per_device(dims, velocity, station_cells, event_cells, delays, active):
    n_src, n_space, ny, nz, events = dims
    rows = ny // (n_space * GROUP)
    tall = rows + 2 * HALO
    peers = n_src // GROUP
    chunk_x = n_space // peers
    own_rows = ny // n_src
    src_rows = rows + 10
    f32 = jnp.float32
    plane = (n_space, nz)
    smem = pl.BlockSpec(memory_space=pltpu.SMEM)
    anywhere = pl.BlockSpec(memory_space=pl.ANY)
    hbm = pl.BlockSpec(memory_space=pltpu.HBM)
    times, kernel_part = pl.pallas_call(
        functools.partial(kernel, dims),
        out_shape=(
            jax.ShapeDtypeStruct((ny, nz), f32),
            jax.ShapeDtypeStruct((own_rows, nz), f32),
        ),
        in_specs=[hbm, smem, smem, hbm, hbm],
        out_specs=(anywhere, anywhere),
        scratch_shapes=[
            pltpu.VMEM((1, 128), f32),
            pltpu.VMEM((3, events), jnp.int32),
            pltpu.VMEM((tall,) + plane, f32),
            pltpu.VMEM((tall,) + plane, f32),
            pltpu.VMEM((GROUP, n_space, 128), f32),
            pltpu.VMEM((GROUP, 1, events), f32),
            pltpu.VMEM((GROUP, tall + 2) + plane, f32),
            pltpu.VMEM((GROUP, tall + 2) + plane, f32),
            pltpu.VMEM((GROUP, tall + 2) + plane, f32),
            pltpu.VMEM((src_rows, 1 + GROUP) + plane, f32),
            pltpu.VMEM((2, GROUP, 3) + plane, f32),
            pltpu.VMEM((GROUP,) + plane, f32),
            pltpu.VMEM((GROUP, 6, src_rows - 2) + plane, f32),
            pltpu.VMEM((GROUP, src_rows) + plane, f32),
            pltpu.VMEM((GROUP, src_rows) + plane, f32),
            pltpu.VMEM((GROUP, src_rows) + plane, f32),
            pltpu.VMEM((rows + 2,) + plane, f32),
            pltpu.VMEM((rows,) + plane, f32),
            pltpu.VMEM((peers, rows, chunk_x, nz), f32),
            pltpu.VMEM((rows, chunk_x, nz), f32),
            pltpu.SemaphoreType.DMA,
            pltpu.SemaphoreType.DMA((8,)),
            pltpu.SemaphoreType.DMA((10,)),
            pltpu.SemaphoreType.DMA((4,)),
            pltpu.SemaphoreType.DMA((4,)),
            pltpu.SemaphoreType.DMA((chunk_x,)),
        ],
        compiler_params=pltpu.CompilerParams(
            collective_id=0, has_side_effects=True, vmem_limit_bytes=60 << 20
        ),
    )(velocity[0], station_cells, active[:, 0, 0, :], event_cells, delays)
    return times[None, None], kernel_part[None]


def solution(mesh):
    n_src, n_space = mesh.shape["src"], mesh.shape["space"]

    def run(velocity, station_cells, event_cells, delays, active):
        dims = (n_src, n_space, velocity.shape[1], velocity.shape[2], event_cells.shape[1])
        return jax.shard_map(
            functools.partial(per_device, dims),
            mesh=mesh,
            in_specs=(
                P("space", None, None),
                P("src", None),
                P(),
                P("src", None),
                P(None, "src", "space", None),
            ),
            out_specs=(P("src", "space", None, None), P("space", "src", None)),
            check_vma=False,
        )(velocity, station_cells, event_cells, delays, active)

    return run
```

```python
import functools

import jax
import jax.numpy as jnp
from jax import lax
from jax.experimental import pallas as pl
from jax.experimental.pallas import tpu as pltpu
from jax.sharding import PartitionSpec as P

TY = 32
BIG = 1000000.0
HALO = 8
GROUP = 2
MESH = pl.DeviceIdType.MESH


def godunov(near_x, near_y, near_z, cost, cost_1, cost_2, cost_3):
    low_xy = jnp.minimum(near_x, near_y)
    high_xy = jnp.maximum(near_x, near_y)
    lowest = jnp.minimum(low_xy, near_z)
    rest = jnp.maximum(low_xy, near_z)
    gap2 = jnp.minimum(high_xy, rest) - lowest
    gap3 = jnp.maximum(high_xy, rest) - lowest
    step = gap3 - gap2
    spread = gap3 * gap3 + step * step
    two = cost_1 <= spread
    disc = jnp.where(two, cost_2, cost_3 - spread) - gap2 * gap2
    base = gap2 + jnp.where(two, 0.0, gap3)
    scale = jnp.where(two, 0.5, 1.0 / 3.0)
    disc = jnp.maximum(disc, 1e-30)
    wide = (base + disc * lax.rsqrt(disc)) * scale
    return lowest + jnp.where(cost <= gap2, cost, wide)


def tiles_of(ref, index):
    return {
        (t, h): ref[index + (pl.ds(8 * t, 8), pl.ds(128 * h, 128))]
        for t in range(ref.shape[-2] // 8)
        for h in range(ref.shape[-1] // 128)
    }


def at_tile(t, h):
    return (pl.ds(8 * t, 8), pl.ds(128 * h, 128))


def beside_x(field, fill):
    sub = lax.broadcasted_iota(jnp.int32, (8, 128), 0)
    down = {key: pltpu.roll(value, 1, 0) for key, value in field.items()}
    up = {key: pltpu.roll(value, 7, 0) for key, value in field.items()}
    low = {(t, h): jnp.where(sub == 0, down.get((t - 1, h), fill), down[t, h]) for t, h in field}
    high = {(t, h): jnp.where(sub == 7, up.get((t + 1, h), fill), up[t, h]) for t, h in field}
    return low, high


def beside_z(field, fill):
    lane = lax.broadcasted_iota(jnp.int32, (8, 128), 1)
    down = {key: pltpu.roll(value, 1, 1) for key, value in field.items()}
    up = {key: pltpu.roll(value, 127, 1) for key, value in field.items()}
    low = {(t, h): jnp.where(lane == 0, down.get((t, h - 1), fill), down[t, h]) for t, h in field}
    high = {(t, h): jnp.where(lane == 127, up.get((t, h + 1), fill), up[t, h]) for t, h in field}
    return low, high


def root(value):
    return value * lax.rsqrt(jnp.maximum(value, 1e-30))


def kernel(
    dims,
    velocity_ref,
    cells_ref,
    flags_ref,
    events_hbm,
    delays_ref,
    times_out,
    kernel_out,
    meta_ref,
    events_ref,
    vel,
    slow,
    meta,
    delay,
    start,
    time_a,
    time_b,
    landed,
    masks,
    spot,
    weights,
    source,
    adj_a,
    adj_b,
    dens,
    part,
    parts,
    total,
    local_sem,
    send_sem,
    recv_sem,
    halo_send,
    halo_recv,
    last_sem,
):
    n_src, n_space, ny, nz, events = dims
    group = GROUP
    rows = ny // (n_space * group)
    peers = n_src // group
    chunk_x = n_space // peers
    own_rows = ny // n_src
    per_owner = own_rows // rows
    tall = rows + 2 * HALO
    s, p = lax.axis_index("src"), lax.axis_index("space")
    m, g = s // group, s % group
    block = g * n_space + p
    y_base = block * rows
    n_blocks = n_space * group

    def where_is(b):
        return (m * group + b // n_space, b % n_space)

    owner = block // per_owner
    targets = [(owner, chunk_x * m + k) for k in range(chunk_x)]
    sources = []
    for k in range(per_owner):
        b = s * per_owner + k
        sources.append(((p // chunk_x) * group + b // n_space, b % n_space))

    fetch_events = pltpu.make_async_copy(events_hbm, events_ref, local_sem)
    fetch_events.start()

    lane = lax.broadcasted_iota(jnp.int32, (1, 128), 1)
    line = jnp.zeros((1, 128), jnp.float32)
    tile_count = ny // TY
    for r in range(2):
        for t in range(tile_count):
            flag = flags_ref[r, t].astype(jnp.float32)
            line = jnp.where(lane == r * tile_count + t, flag, line)
    for d in range(3):
        line = jnp.where(lane == 64 + d, cells_ref[0, d].astype(jnp.float32), line)
    meta_ref[...] = line

    barrier = pltpu.get_barrier_semaphore()
    signals = 0
    for i in range(1, n_space):
        to = (s, (p + i) % n_space)
        pl.semaphore_signal(barrier, inc=1, device_id=to, device_id_type=MESH)
        signals += 1
    for dg in range(1, group):
        to = (m * group + (g + dg) % group, p)
        pl.semaphore_signal(barrier, inc=1, device_id=to, device_id_type=MESH)
        signals += 1
    for i in range(1, peers):
        to = (((m + i) % peers) * group + g, p)
        pl.semaphore_signal(barrier, inc=1, device_id=to, device_id_type=MESH)
        signals += 1
    for to in sources:
        mine = (to[0] == s) & (to[1] == p)

        @pl.when(jnp.logical_not(mine))
        def _():
            pl.semaphore_signal(barrier, inc=1, device_id=to, device_id_type=MESH)

        signals = signals + jnp.where(mine, 0, 1)
    pl.semaphore_wait(barrier, signals)

    own = pl.ds(HALO, rows)
    partners = [(m * group + (g + dg) % group, p) for dg in range(1, group)]
    for i in range(n_space):
        q = (p + i) % n_space
        line = meta.at[g, pl.ds(p, 1), :]
        if i == 0:
            pltpu.make_async_copy(meta_ref, line, recv_sem.at[1]).start()
        else:
            pltpu.make_async_remote_copy(
                meta_ref,
                line,
                send_sem.at[1],
                recv_sem.at[1],
                device_id=(s, q),
                device_id_type=MESH,
            ).start()
    half = n_space // 2
    near_half = (p // half) * half
    far_half = half - near_half
    for i in range(n_space):
        if i < half:
            q = near_half + (p + i) % half
        else:
            q = far_half + (p + i) % half
        piece = velocity_ref.at[pl.ds(pl.multiple_of((g * n_space + q) * rows, 8), rows), :]
        arrived = recv_sem.at[0] if i < half else recv_sem.at[9]
        if i == 0:
            pltpu.make_async_copy(piece, vel.at[own, p, :], arrived).start()
        else:
            pltpu.make_async_remote_copy(
                piece,
                vel.at[own, p, :],
                send_sem.at[0],
                arrived,
                device_id=(s, q),
                device_id_type=MESH,
            ).start()
    pltpu.make_async_copy(delays_ref, delay.at[g], recv_sem.at[2]).start()
    for to in partners:
        pltpu.make_async_remote_copy(
            delays_ref,
            delay.at[g],
            send_sem.at[2],
            recv_sem.at[2],
            device_id=to,
            device_id_type=MESH,
        ).start()

    src_rows = rows + 10
    cells = rows * n_space
    step_events = 1024
    steps = events // step_events
    mine_rows = pl.ds(5, rows)
    landed[mine_rows] = jnp.zeros((rows, 1 + group, n_space, nz), jnp.float32)
    fetch_events.wait()
    pltpu.make_async_copy(delay, delay, recv_sem.at[2]).wait()

    def add_events(c, carry):
        at = pl.ds(pl.multiple_of(c * step_events, step_events), step_events)
        event_x = events_ref[0:1, at]
        event_y = events_ref[1:2, at]
        event_z = events_ref[2:3, at]
        key = (event_y - y_base) * n_space + event_x
        cell = lax.broadcasted_iota(jnp.int32, (cells, step_events), 0)
        left = jnp.where(cell == key, 1.0, 0.0).astype(jnp.bfloat16)
        deep = lax.broadcasted_iota(jnp.int32, (nz, step_events), 0) == event_z
        contract = (((1,), (1,)), ((), ()))

        def product(value):
            right = jnp.where(deep, value, 0.0).astype(jnp.bfloat16)
            out = lax.dot_general(left, right, contract, preferred_element_type=jnp.float32)
            return out.reshape(rows, n_space, nz)

        landed[mine_rows, 0] += product(1.0)
        for k in range(group):
            lateness = delay[k, 0:1, at]
            coarse = lateness.astype(jnp.bfloat16).astype(jnp.float32)
            landed[mine_rows, 1 + k] += product(coarse) + product(lateness - coarse)
        return carry

    wide_lane = lax.broadcasted_iota(jnp.int32, (n_space, 128), 1)
    layer_f = lax.broadcasted_iota(jnp.int32, (n_space, nz), 0).astype(jnp.float32)
    depth_f = lax.broadcasted_iota(jnp.int32, (n_space, nz), 1).astype(jnp.float32)
    first_tile = (y_base - HALO + TY) // TY - 1

    def column(k, index):
        picked = jnp.where(wide_lane == index, meta[k], 0.0)
        return jnp.broadcast_to(jnp.sum(picked, axis=1, keepdims=True), (n_space, nz))

    def row_valid(y):
        return (y >= 0) & (y < ny)

    def init_fields():
        for dg in range(1, group):
            other = (g + dg) % group
            pltpu.make_async_copy(meta.at[other], meta.at[other], recv_sem.at[3]).wait()
        for k in range(group):
            for r in range(2):
                for t in range(2):
                    masks[r, k, t] = column(k, r * tile_count + first_tile + t)
                masks[r, k, 2] = jnp.zeros((n_space, nz), jnp.float32)
            cell_x, cell_y, cell_z = column(k, 64), column(k, 65), column(k, 66)
            here = (layer_f == cell_x) & (depth_f == cell_z)
            spot[k] = jnp.where(here, cell_y, -1.0)
            off_x, off_z = layer_f - cell_x, depth_f - cell_z
            flat = off_x * off_x + off_z * off_z

            def init_row(j, carry):
                y = y_base - HALO - 1 + j
                diff = y.astype(jnp.float32) - cell_y
                start[k, j] = jnp.where(row_valid(y), root(flat + diff * diff), BIG)
                return carry

            lax.fori_loop(0, tall + 2, init_row, 0, unroll=2)

    before = where_is((block + n_blocks - 1) % n_blocks)
    after = where_is((block + 1) % n_blocks)
    cut = steps // 2
    lax.fori_loop(0, cut, add_events, 0)

    pltpu.make_async_copy(meta.at[g], meta.at[g], recv_sem.at[1]).wait()
    for to in partners:
        pltpu.make_async_remote_copy(
            meta.at[g],
            meta.at[g],
            send_sem.at[3],
            recv_sem.at[3],
            device_id=to,
            device_id_type=MESH,
        ).start()
    lax.fori_loop(cut, steps, add_events, 0)

    halos = []
    for n, (x_at, arrived) in enumerate(((near_half, 0), (far_half, 9))):
        layers = pl.ds(pl.multiple_of(x_at, half), half)
        here = vel.at[own, layers, :]
        pltpu.make_async_copy(here, here, recv_sem.at[arrived]).wait()
        for d, (at, there, to) in enumerate(
            ((HALO, HALO + rows, before), (rows, 0, after))
        ):
            halo = pltpu.make_async_remote_copy(
                vel.at[pl.ds(at, HALO), layers, :],
                vel.at[pl.ds(there, HALO), layers, :],
                halo_send.at[2 * n + d],
                halo_recv.at[2 * n + d],
                device_id=to,
                device_id_type=MESH,
            )
            halo.start()
            halos.append(halo)
        if n == 0:
            init_fields()

    events_before = pltpu.make_async_remote_copy(
        landed.at[pl.ds(5, 5)],
        landed.at[pl.ds(5 + rows, 5)],
        send_sem.at[4],
        recv_sem.at[4],
        device_id=before,
        device_id_type=MESH,
    )
    events_after = pltpu.make_async_remote_copy(
        landed.at[pl.ds(rows, 5)],
        landed.at[pl.ds(0, 5)],
        send_sem.at[5],
        recv_sem.at[5],
        device_id=after,
        device_id_type=MESH,
    )

    def slow_row(j, carry):
        slow[j] = 1.0 / vel[j]
        return carry

    def sweep_row(old, new, r, j):
        y = y_base - HALO + j
        kind = jnp.where(row_valid(y), (y + TY) // TY - 1 - first_tile, 2)
        level = y.astype(jnp.float32)
        centre = [tiles_of(old, (k, j + 1)) for k in range(group)]
        near_x = [beside_x(field, BIG) for field in centre]
        near_z = [beside_z(field, BIG) for field in centre]
        for t, h in centre[0]:
            tile = at_tile(t, h)
            cost = slow[(j,) + tile]
            cost_1 = cost * cost
            cost_2 = cost_1 + cost_1
            cost_3 = cost_2 + cost_1
            for k in range(group):
                update = godunov(
                    jnp.minimum(near_x[k][0][t, h], near_x[k][1][t, h]),
                    jnp.minimum(old[(k, j) + tile], old[(k, j + 2) + tile]),
                    jnp.minimum(near_z[k][0][t, h], near_z[k][1][t, h]),
                    cost,
                    cost_1,
                    cost_2,
                    cost_3,
                )
                chosen = (masks[(r, k, kind) + tile] > 0.0) & (spot[(k,) + tile] != level)
                new[(k, j + 1) + tile] = jnp.where(chosen, update, centre[k][t, h])

    stages = ((start, time_a, 0), (time_a, time_b, 0), (time_b, time_a, 1), (time_a, time_b, 1))
    lax.fori_loop(HALO, HALO + rows, slow_row, 0, unroll=4)
    for n, (old, new, r) in enumerate(stages):

        def inside(j, carry):
            sweep_row(old, new, r, j)
            return carry

        lax.fori_loop(HALO + n, HALO + rows - n, inside, 0, unroll=2)

    for halo in halos:
        halo.wait_recv()
    events_before.start()
    events_after.start()
    lax.fori_loop(0, HALO, slow_row, 0, unroll=4)
    lax.fori_loop(HALO + rows, tall, slow_row, 0, unroll=4)
    for n, (old, new, r) in enumerate(stages):

        def outside(i, carry):
            sweep_row(old, new, r, n + i)
            sweep_row(old, new, r, HALO + rows - n + i)
            return carry

        lax.fori_loop(0, HALO, outside, 0, unroll=2)

    inner = pl.ds(HALO + 1, rows)

    def send_times(k):
        for i in range(n_space):
            q = (p + i) % n_space
            piece = time_b.at[k, inner, q, :]
            place = times_out.at[pl.ds(pl.multiple_of(y_base, 8), rows), :]
            to_src = m * group + k

            def send(piece=piece, place=place, to_src=to_src, q=q):
                pltpu.make_async_remote_copy(
                    piece,
                    place,
                    send_sem.at[6],
                    recv_sem.at[6],
                    device_id=(to_src, q),
                    device_id_type=MESH,
                ).start()

            if i:
                send()
            else:

                @pl.when(g == k)
                def _():
                    pltpu.make_async_copy(piece, place, recv_sem.at[6]).start()

                @pl.when(g != k)
                def _():
                    send()

    send_times(0)

    def weight_row(i, carry):
        j = i + 5
        for k in range(group):
            centre = tiles_of(time_b, (k, j))
            x_low, x_high = beside_x(centre, 0.0)
            z_low, z_high = beside_z(centre, 0.0)
            for t, h in centre:
                tile = at_tile(t, h)
                rate = vel[(i + 4,) + tile] * (1.0 / 6.0)
                around = (
                    x_low[t, h],
                    x_high[t, h],
                    time_b[(k, j - 1) + tile],
                    time_b[(k, j + 1) + tile],
                    z_low[t, h],
                    z_high[t, h],
                )
                for d, near in enumerate(around):
                    weights[(k, d, i) + tile] = jnp.maximum(near - centre[t, h], 0.0) * rate
        return carry

    lax.fori_loop(0, src_rows - 2, weight_row, 0, unroll=4)

    events_before.wait_recv()
    events_after.wait_recv()

    def source_row(i, carry):
        valid = row_valid(y_base - 5 + i)
        for k in range(group):
            shift = time_b[k, i + 4] - start[k, i + 4]
            value = landed[i, 0] * shift - landed[i, 1 + k]
            source[k, i] = jnp.where(valid, value, 0.0)
        return carry

    lax.fori_loop(0, src_rows, source_row, 0, unroll=2)

    def adjoint_sweep(old, new, low, high):
        def row(i, carry):
            for k in range(group):
                centre = tiles_of(old, (k, i))
                x_low, x_high = beside_x(centre, 0.0)
                z_low, z_high = beside_z(centre, 0.0)
                for t, h in centre:
                    tile = at_tile(t, h)
                    weight = [weights[(k, d, i - 1) + tile] for d in range(6)]
                    along_x = weight[0] * x_low[t, h] + weight[1] * x_high[t, h]
                    along_y = weight[2] * old[(k, i - 1) + tile] + weight[3] * old[(k, i + 1) + tile]
                    along_z = weight[4] * z_low[t, h] + weight[5] * z_high[t, h]
                    new[(k, i) + tile] = source[(k, i) + tile] + along_x + (along_y + along_z)
            return carry

        lax.fori_loop(low, high, row, 0, unroll=4)

    adjoint_sweep(source, adj_a, 1, src_rows - 1)
    adjoint_sweep(adj_a, adj_b, 2, src_rows - 2)
    adjoint_sweep(adj_b, adj_a, 3, src_rows - 3)
    adjoint_sweep(adj_a, adj_b, 4, src_rows - 4)

    def density_row(i, carry):
        value = adj_b[0, i + 4]
        for k in range(1, group):
            value = value + adj_b[k, i + 4]
        dens[i] = slow[i + HALO - 1] * value
        return carry

    lax.fori_loop(0, rows + 2, density_row, 0, unroll=2)

    def smooth_row(i, carry):
        first, middle, last = (tiles_of(dens, (i + d,)) for d in range(3))
        value = {key: first[key] + 2.0 * middle[key] + last[key] for key in first}
        for beside in (beside_x, beside_z):
            low, high = beside(value, 0.0)
            value = {key: low[key] + 2.0 * value[key] + high[key] for key in value}
        for t, h in value:
            part[(i,) + at_tile(t, h)] = value[t, h] * (1.0 / 64.0)
        return carry

    lax.fori_loop(0, rows, smooth_row, 0, unroll=2)

    for i in range(peers):
        q = (m + i) % peers
        piece = part.at[:, pl.ds(pl.multiple_of(q * chunk_x, chunk_x), chunk_x), :]
        if i == 0:
            pltpu.make_async_copy(piece, parts.at[m], recv_sem.at[7]).start()
        else:
            pltpu.make_async_remote_copy(
                piece,
                parts.at[m],
                send_sem.at[7],
                recv_sem.at[7],
                device_id=(q * group + g, p),
                device_id_type=MESH,
            ).start()
    for k in range(1, group):
        send_times(k)
    pltpu.make_async_copy(parts, parts, recv_sem.at[7]).wait()
    summed = parts[0]
    for i in range(1, peers):
        summed = summed + parts[i]
    total[...] = summed
    place_k = block % per_owner
    for k in range(chunk_x):
        to = targets[k]
        piece = total.at[:, k, :]
        place = kernel_out.at[pl.ds(pl.multiple_of(place_k * rows, 8), rows), :]
        mine = (to[0] == s) & (to[1] == p)

        @pl.when(mine)
        def _():
            pltpu.make_async_copy(piece, place, recv_sem.at[8]).start()

        @pl.when(jnp.logical_not(mine))
        def _():
            pltpu.make_async_remote_copy(
                piece,
                place,
                last_sem.at[k],
                recv_sem.at[8],
                device_id=to,
                device_id_type=MESH,
            ).start()

    def drain(ref, sem):
        pltpu.make_async_copy(ref, ref, sem).wait()

    drain(velocity_ref.at[pl.ds(0, (n_space - 1) * rows), :], send_sem.at[0])
    drain(meta.at[0, pl.ds(0, n_space - 8), :], send_sem.at[1])
    for _ in range(7):
        drain(meta_ref, send_sem.at[1])
    for _ in partners:
        drain(delay.at[0], send_sem.at[2])
        drain(meta.at[0], send_sem.at[3])
    for halo in halos:
        halo.wait_send()
    events_before.wait_send()
    events_after.wait_send()
    drain(times_out.at[pl.ds(0, (n_blocks - 1) * rows), :], send_sem.at[6])
    drain(parts.at[pl.ds(1, peers - 1)], send_sem.at[7])
    for k in range(chunk_x):
        to = targets[k]
        mine = (to[0] == s) & (to[1] == p)

        @pl.when(jnp.logical_not(mine))
        def _():
            drain(total.at[:, k, :], last_sem.at[k])

    drain(times_out, recv_sem.at[6])
    drain(kernel_out, recv_sem.at[8])


def per_device(dims, velocity, station_cells, event_cells, delays, active):
    n_src, n_space, ny, nz, events = dims
    rows = ny // (n_space * GROUP)
    tall = rows + 2 * HALO
    peers = n_src // GROUP
    chunk_x = n_space // peers
    own_rows = ny // n_src
    src_rows = rows + 10
    f32 = jnp.float32
    plane = (n_space, nz)
    smem = pl.BlockSpec(memory_space=pltpu.SMEM)
    anywhere = pl.BlockSpec(memory_space=pl.ANY)
    hbm = pl.BlockSpec(memory_space=pltpu.HBM)
    times, kernel_part = pl.pallas_call(
        functools.partial(kernel, dims),
        out_shape=(
            jax.ShapeDtypeStruct((ny, nz), f32),
            jax.ShapeDtypeStruct((own_rows, nz), f32),
        ),
        in_specs=[hbm, smem, smem, hbm, hbm],
        out_specs=(anywhere, anywhere),
        scratch_shapes=[
            pltpu.VMEM((1, 128), f32),
            pltpu.VMEM((3, events), jnp.int32),
            pltpu.VMEM((tall,) + plane, f32),
            pltpu.VMEM((tall,) + plane, f32),
            pltpu.VMEM((GROUP, n_space, 128), f32),
            pltpu.VMEM((GROUP, 1, events), f32),
            pltpu.VMEM((GROUP, tall + 2) + plane, f32),
            pltpu.VMEM((GROUP, tall + 2) + plane, f32),
            pltpu.VMEM((GROUP, tall + 2) + plane, f32),
            pltpu.VMEM((src_rows, 1 + GROUP) + plane, f32),
            pltpu.VMEM((2, GROUP, 3) + plane, f32),
            pltpu.VMEM((GROUP,) + plane, f32),
            pltpu.VMEM((GROUP, 6, src_rows - 2) + plane, f32),
            pltpu.VMEM((GROUP, src_rows) + plane, f32),
            pltpu.VMEM((GROUP, src_rows) + plane, f32),
            pltpu.VMEM((GROUP, src_rows) + plane, f32),
            pltpu.VMEM((rows + 2,) + plane, f32),
            pltpu.VMEM((rows,) + plane, f32),
            pltpu.VMEM((peers, rows, chunk_x, nz), f32),
            pltpu.VMEM((rows, chunk_x, nz), f32),
            pltpu.SemaphoreType.DMA,
            pltpu.SemaphoreType.DMA((8,)),
            pltpu.SemaphoreType.DMA((10,)),
            pltpu.SemaphoreType.DMA((4,)),
            pltpu.SemaphoreType.DMA((4,)),
            pltpu.SemaphoreType.DMA((chunk_x,)),
        ],
        compiler_params=pltpu.CompilerParams(
            collective_id=0, has_side_effects=True, vmem_limit_bytes=48 << 20
        ),
    )(
        *(
            pltpu.with_memory_space_constraint(array, pltpu.HBM)
            for array in (velocity[0], station_cells, active[:, 0, 0, :], event_cells, delays)
        )
    )
    return times[None, None], kernel_part[None]


def solution(mesh):
    n_src, n_space = mesh.shape["src"], mesh.shape["space"]

    def run(velocity, station_cells, event_cells, delays, active):
        dims = (n_src, n_space, velocity.shape[1], velocity.shape[2], event_cells.shape[1])
        return jax.shard_map(
            functools.partial(per_device, dims),
            mesh=mesh,
            in_specs=(
                P("space", None, None),
                P("src", None),
                P(),
                P("src", None),
                P(None, "src", "space", None),
            ),
            out_specs=(P("src", "space", None, None), P("space", "src", None)),
            check_vma=False,
        )(velocity, station_cells, event_cells, delays, active)

    return run
```

```python
import functools

import jax
import jax.numpy as jnp
from jax import lax
from jax.experimental import pallas as pl
from jax.experimental.pallas import tpu as pltpu
from jax.sharding import PartitionSpec as P

TY = 32
BIG = 1000000.0
HALO = 8
GROUP = 2
MESH = pl.DeviceIdType.MESH


def godunov(near_x, near_y, near_z, cost, cost_1, cost_2, cost_3):
    low_xy = jnp.minimum(near_x, near_y)
    high_xy = jnp.maximum(near_x, near_y)
    lowest = jnp.minimum(low_xy, near_z)
    rest = jnp.maximum(low_xy, near_z)
    gap2 = jnp.minimum(high_xy, rest) - lowest
    gap3 = jnp.maximum(high_xy, rest) - lowest
    step = gap3 - gap2
    spread = gap3 * gap3 + step * step
    two = cost_1 <= spread
    disc = jnp.where(two, cost_2, cost_3 - spread) - gap2 * gap2
    base = gap2 + jnp.where(two, 0.0, gap3)
    scale = jnp.where(two, 0.5, 1.0 / 3.0)
    disc = jnp.maximum(disc, 1e-30)
    wide = (base + disc * lax.rsqrt(disc)) * scale
    return lowest + jnp.where(cost <= gap2, cost, wide)


def tiles_of(ref, index):
    return {
        (t, h): ref[index + (pl.ds(8 * t, 8), pl.ds(128 * h, 128))]
        for t in range(ref.shape[-2] // 8)
        for h in range(ref.shape[-1] // 128)
    }


def at_tile(t, h):
    return (pl.ds(8 * t, 8), pl.ds(128 * h, 128))


def beside_x(field, fill):
    sub = lax.broadcasted_iota(jnp.int32, (8, 128), 0)
    down = {key: pltpu.roll(value, 1, 0) for key, value in field.items()}
    up = {key: pltpu.roll(value, 7, 0) for key, value in field.items()}
    low = {(t, h): jnp.where(sub == 0, down.get((t - 1, h), fill), down[t, h]) for t, h in field}
    high = {(t, h): jnp.where(sub == 7, up.get((t + 1, h), fill), up[t, h]) for t, h in field}
    return low, high


def beside_z(field, fill):
    lane = lax.broadcasted_iota(jnp.int32, (8, 128), 1)
    down = {key: pltpu.roll(value, 1, 1) for key, value in field.items()}
    up = {key: pltpu.roll(value, 127, 1) for key, value in field.items()}
    low = {(t, h): jnp.where(lane == 0, down.get((t, h - 1), fill), down[t, h]) for t, h in field}
    high = {(t, h): jnp.where(lane == 127, up.get((t, h + 1), fill), up[t, h]) for t, h in field}
    return low, high


def root(value):
    return value * lax.rsqrt(jnp.maximum(value, 1e-30))


def kernel(
    dims,
    velocity_ref,
    cells_ref,
    flags_ref,
    events_hbm,
    delays_ref,
    times_out,
    kernel_out,
    meta_ref,
    events_ref,
    vel,
    slow,
    meta,
    delay,
    start,
    time_a,
    time_b,
    count,
    landed,
    left,
    masks,
    spot,
    weights,
    source,
    adj_a,
    adj_b,
    dens,
    part,
    parts,
    total,
    local_sem,
    send_sem,
    recv_sem,
    halo_send,
    halo_recv,
    event_send,
    event_recv,
    last_sem,
):
    n_src, n_space, ny, nz, events = dims
    group = GROUP
    rows = ny // (n_space * group)
    peers = n_src // group
    chunk_x = n_space // peers
    own_rows = ny // n_src
    per_owner = own_rows // rows
    tall = rows + 2 * HALO
    s, p = lax.axis_index("src"), lax.axis_index("space")
    m, g = s // group, s % group
    block = g * n_space + p
    y_base = block * rows
    n_blocks = n_space * group

    def where_is(b):
        return (m * group + b // n_space, b % n_space)

    owner = block // per_owner
    targets = [(owner, chunk_x * m + k) for k in range(chunk_x)]
    sources = []
    for k in range(per_owner):
        b = s * per_owner + k
        sources.append(((p // chunk_x) * group + b // n_space, b % n_space))

    fetch_events = pltpu.make_async_copy(events_hbm, events_ref, local_sem)
    fetch_events.start()

    lane = lax.broadcasted_iota(jnp.int32, (1, 128), 1)
    line = jnp.zeros((1, 128), jnp.float32)
    tile_count = ny // TY
    for r in range(2):
        for t in range(tile_count):
            flag = flags_ref[r, t].astype(jnp.float32)
            line = jnp.where(lane == r * tile_count + t, flag, line)
    for d in range(3):
        line = jnp.where(lane == 64 + d, cells_ref[0, d].astype(jnp.float32), line)
    meta_ref[...] = line

    barrier = pltpu.get_barrier_semaphore()
    signals = 0
    for i in range(1, n_space):
        to = (s, (p + i) % n_space)
        pl.semaphore_signal(barrier, inc=1, device_id=to, device_id_type=MESH)
        signals += 1
    for dg in range(1, group):
        to = (m * group + (g + dg) % group, p)
        pl.semaphore_signal(barrier, inc=1, device_id=to, device_id_type=MESH)
        signals += 1
    for i in range(1, peers):
        to = (((m + i) % peers) * group + g, p)
        pl.semaphore_signal(barrier, inc=1, device_id=to, device_id_type=MESH)
        signals += 1
    for to in sources:
        mine = (to[0] == s) & (to[1] == p)

        @pl.when(jnp.logical_not(mine))
        def _():
            pl.semaphore_signal(barrier, inc=1, device_id=to, device_id_type=MESH)

        signals = signals + jnp.where(mine, 0, 1)

    src_rows = rows + 10
    cells = rows * n_space
    step_events = 2048
    steps = events // step_events
    contract = (((1,), (1,)), ((), ()))
    mine_rows = pl.ds(5, rows)
    count[mine_rows] = jnp.zeros((rows, n_space, nz), jnp.float32)
    fetch_events.wait()

    def product(first, second):
        out = lax.dot_general(first, second, contract, preferred_element_type=jnp.float32)
        return out.reshape(rows, n_space, nz)

    def depth_of(at):
        deep = lax.broadcasted_iota(jnp.int32, (nz, step_events), 0)
        return deep == events_ref[2:3, at]

    def count_events(c, carry):
        at = pl.ds(pl.multiple_of(c * step_events, step_events), step_events)
        key = (events_ref[1:2, at] - y_base) * n_space + events_ref[0:1, at]
        cell = lax.broadcasted_iota(jnp.int32, (cells, step_events), 0)
        left[:, at] = jnp.where(cell == key, 1.0, 0.0).astype(jnp.bfloat16)
        right = jnp.where(depth_of(at), 1.0, 0.0).astype(jnp.bfloat16)
        count[mine_rows] += product(left[:, at], right)
        return carry

    lax.fori_loop(0, steps, count_events, 0)
    pl.semaphore_wait(barrier, signals)

    own = pl.ds(HALO, rows)
    partners = [(m * group + (g + dg) % group, p) for dg in range(1, group)]
    for i in range(n_space):
        q = (p + i) % n_space
        line = meta.at[g, pl.ds(p, 1), :]
        if i == 0:
            pltpu.make_async_copy(meta_ref, line, recv_sem.at[1]).start()
        else:
            pltpu.make_async_remote_copy(
                meta_ref,
                line,
                send_sem.at[1],
                recv_sem.at[1],
                device_id=(s, q),
                device_id_type=MESH,
            ).start()
    half = n_space // 2
    near_half = (p // half) * half
    far_half = half - near_half
    for i in range(n_space):
        if i < half:
            q = near_half + (p + i) % half
        else:
            q = far_half + (p + i) % half
        piece = velocity_ref.at[pl.ds(pl.multiple_of((g * n_space + q) * rows, 8), rows), :]
        arrived = recv_sem.at[0] if i < half else recv_sem.at[9]
        if i == 0:
            pltpu.make_async_copy(piece, vel.at[own, p, :], arrived).start()
        else:
            pltpu.make_async_remote_copy(
                piece,
                vel.at[own, p, :],
                send_sem.at[0],
                arrived,
                device_id=(s, q),
                device_id_type=MESH,
            ).start()
    pltpu.make_async_copy(delays_ref, delay.at[g], recv_sem.at[2]).start()
    for to in partners:
        pltpu.make_async_remote_copy(
            delays_ref,
            delay.at[g],
            send_sem.at[2],
            recv_sem.at[2],
            device_id=to,
            device_id_type=MESH,
        ).start()

    before = where_is((block + n_blocks - 1) % n_blocks)
    after = where_is((block + 1) % n_blocks)

    def event_halo(ref, n, to):
        at, there = ((5, 5 + rows), (rows, 0))[n % 2]
        return pltpu.make_async_remote_copy(
            ref.at[pl.ds(at, 5)],
            ref.at[pl.ds(there, 5)],
            event_send.at[n],
            event_recv.at[n],
            device_id=to,
            device_id_type=MESH,
        )

    pltpu.make_async_copy(delay, delay, recv_sem.at[2]).wait()
    event_halos = [event_halo(count, 0, before), event_halo(count, 1, after)]
    for halo in event_halos:
        halo.start()

    landed[mine_rows] = jnp.zeros((rows, group, n_space, nz), jnp.float32)

    def add_events(c, carry):
        at = pl.ds(pl.multiple_of(c * step_events, step_events), step_events)
        deep = depth_of(at)
        for k in range(group):
            lateness = delay[k, 0:1, at]
            coarse = lateness.astype(jnp.bfloat16).astype(jnp.float32)
            for value in (coarse, lateness - coarse):
                right = jnp.where(deep, value, 0.0).astype(jnp.bfloat16)
                landed[mine_rows, k] += product(left[:, at], right)
        return carry

    wide_lane = lax.broadcasted_iota(jnp.int32, (n_space, 128), 1)
    layer_f = lax.broadcasted_iota(jnp.int32, (n_space, nz), 0).astype(jnp.float32)
    depth_f = lax.broadcasted_iota(jnp.int32, (n_space, nz), 1).astype(jnp.float32)
    first_tile = (y_base - HALO + TY) // TY - 1

    def column(k, index):
        picked = jnp.where(wide_lane == index, meta[k], 0.0)
        return jnp.broadcast_to(jnp.sum(picked, axis=1, keepdims=True), (n_space, nz))

    def row_valid(y):
        return (y >= 0) & (y < ny)

    def init_fields():
        for dg in range(1, group):
            other = (g + dg) % group
            pltpu.make_async_copy(meta.at[other], meta.at[other], recv_sem.at[3]).wait()
        for k in range(group):
            for r in range(2):
                for t in range(2):
                    masks[r, k, t] = column(k, r * tile_count + first_tile + t)
                masks[r, k, 2] = jnp.zeros((n_space, nz), jnp.float32)
            cell_x, cell_y, cell_z = column(k, 64), column(k, 65), column(k, 66)
            here = (layer_f == cell_x) & (depth_f == cell_z)
            spot[k] = jnp.where(here, cell_y, -1.0)
            off_x, off_z = layer_f - cell_x, depth_f - cell_z
            flat = off_x * off_x + off_z * off_z

            def init_row(j, carry):
                y = y_base - HALO - 1 + j
                diff = y.astype(jnp.float32) - cell_y
                start[k, j] = jnp.where(row_valid(y), root(flat + diff * diff), BIG)
                return carry

            lax.fori_loop(0, tall + 2, init_row, 0, unroll=2)

    cut = steps // 2
    lax.fori_loop(0, cut, add_events, 0)

    pltpu.make_async_copy(meta.at[g], meta.at[g], recv_sem.at[1]).wait()
    for to in partners:
        pltpu.make_async_remote_copy(
            meta.at[g],
            meta.at[g],
            send_sem.at[3],
            recv_sem.at[3],
            device_id=to,
            device_id_type=MESH,
        ).start()
    lax.fori_loop(cut, steps, add_events, 0)

    halos = []
    for n, (x_at, arrived) in enumerate(((near_half, 0), (far_half, 9))):
        layers = pl.ds(pl.multiple_of(x_at, half), half)
        here = vel.at[own, layers, :]
        pltpu.make_async_copy(here, here, recv_sem.at[arrived]).wait()
        for d, (at, there, to) in enumerate(
            ((HALO, HALO + rows, before), (rows, 0, after))
        ):
            halo = pltpu.make_async_remote_copy(
                vel.at[pl.ds(at, HALO), layers, :],
                vel.at[pl.ds(there, HALO), layers, :],
                halo_send.at[2 * n + d],
                halo_recv.at[2 * n + d],
                device_id=to,
                device_id_type=MESH,
            )
            halo.start()
            halos.append(halo)
        if n == 0:
            init_fields()

    for n, to in ((2, before), (3, after)):
        halo = event_halo(landed, n, to)
        halo.start()
        event_halos.append(halo)

    def slow_row(j, carry):
        slow[j] = 1.0 / vel[j]
        return carry

    def sweep_row(old, new, r, j):
        y = y_base - HALO + j
        kind = jnp.where(row_valid(y), (y + TY) // TY - 1 - first_tile, 2)
        level = y.astype(jnp.float32)
        centre = [tiles_of(old, (k, j + 1)) for k in range(group)]
        near_x = [beside_x(field, BIG) for field in centre]
        near_z = [beside_z(field, BIG) for field in centre]
        for t, h in centre[0]:
            tile = at_tile(t, h)
            cost = slow[(j,) + tile]
            cost_1 = cost * cost
            cost_2 = cost_1 + cost_1
            cost_3 = cost_2 + cost_1
            for k in range(group):
                update = godunov(
                    jnp.minimum(near_x[k][0][t, h], near_x[k][1][t, h]),
                    jnp.minimum(old[(k, j) + tile], old[(k, j + 2) + tile]),
                    jnp.minimum(near_z[k][0][t, h], near_z[k][1][t, h]),
                    cost,
                    cost_1,
                    cost_2,
                    cost_3,
                )
                chosen = (masks[(r, k, kind) + tile] > 0.0) & (spot[(k,) + tile] != level)
                new[(k, j + 1) + tile] = jnp.where(chosen, update, centre[k][t, h])

    stages = ((start, time_a, 0), (time_a, time_b, 0), (time_b, time_a, 1), (time_a, time_b, 1))
    lax.fori_loop(HALO, HALO + rows, slow_row, 0, unroll=4)
    for n, (old, new, r) in enumerate(stages):

        def inside(j, carry):
            sweep_row(old, new, r, j)
            return carry

        lax.fori_loop(HALO + n, HALO + rows - n, inside, 0, unroll=2)

    for halo in halos:
        halo.wait_recv()
    lax.fori_loop(0, HALO, slow_row, 0, unroll=4)
    lax.fori_loop(HALO + rows, tall, slow_row, 0, unroll=4)
    for n, (old, new, r) in enumerate(stages):

        def outside(i, carry):
            sweep_row(old, new, r, n + i)
            sweep_row(old, new, r, HALO + rows - n + i)
            return carry

        lax.fori_loop(0, HALO, outside, 0, unroll=4)

    inner = pl.ds(HALO + 1, rows)

    def send_times(k):
        for i in range(n_space):
            q = (p + i) % n_space
            piece = time_b.at[k, inner, q, :]
            place = times_out.at[pl.ds(pl.multiple_of(y_base, 8), rows), :]
            to_src = m * group + k

            def send(piece=piece, place=place, to_src=to_src, q=q):
                pltpu.make_async_remote_copy(
                    piece,
                    place,
                    send_sem.at[6],
                    recv_sem.at[6],
                    device_id=(to_src, q),
                    device_id_type=MESH,
                ).start()

            if i:
                send()
            else:

                @pl.when(g == k)
                def _():
                    pltpu.make_async_copy(piece, place, recv_sem.at[6]).start()

                @pl.when(g != k)
                def _():
                    send()

    send_times(0)

    def weight_row(i, carry):
        j = i + 5
        for k in range(group):
            centre = tiles_of(time_b, (k, j))
            x_low, x_high = beside_x(centre, 0.0)
            z_low, z_high = beside_z(centre, 0.0)
            for t, h in centre:
                tile = at_tile(t, h)
                rate = vel[(i + 4,) + tile] * (1.0 / 6.0)
                around = (
                    x_low[t, h],
                    x_high[t, h],
                    time_b[(k, j - 1) + tile],
                    time_b[(k, j + 1) + tile],
                    z_low[t, h],
                    z_high[t, h],
                )
                for d, near in enumerate(around):
                    weights[(k, d, i) + tile] = jnp.maximum(near - centre[t, h], 0.0) * rate
        return carry

    lax.fori_loop(0, src_rows - 2, weight_row, 0, unroll=4)

    for halo in event_halos:
        halo.wait_recv()

    def source_row(i, carry):
        valid = row_valid(y_base - 5 + i)
        for k in range(group):
            shift = time_b[k, i + 4] - start[k, i + 4]
            value = count[i] * shift - landed[i, k]
            source[k, i] = jnp.where(valid, value, 0.0)
        return carry

    lax.fori_loop(0, src_rows, source_row, 0, unroll=2)

    def adjoint_sweep(old, new, low, high):
        def row(i, carry):
            for k in range(group):
                centre = tiles_of(old, (k, i))
                x_low, x_high = beside_x(centre, 0.0)
                z_low, z_high = beside_z(centre, 0.0)
                for t, h in centre:
                    tile = at_tile(t, h)
                    weight = [weights[(k, d, i - 1) + tile] for d in range(6)]
                    along_x = weight[0] * x_low[t, h] + weight[1] * x_high[t, h]
                    along_y = weight[2] * old[(k, i - 1) + tile] + weight[3] * old[(k, i + 1) + tile]
                    along_z = weight[4] * z_low[t, h] + weight[5] * z_high[t, h]
                    new[(k, i) + tile] = source[(k, i) + tile] + along_x + (along_y + along_z)
            return carry

        lax.fori_loop(low, high, row, 0, unroll=4)

    adjoint_sweep(source, adj_a, 1, src_rows - 1)
    adjoint_sweep(adj_a, adj_b, 2, src_rows - 2)
    adjoint_sweep(adj_b, adj_a, 3, src_rows - 3)
    adjoint_sweep(adj_a, adj_b, 4, src_rows - 4)

    def density_row(i, carry):
        value = adj_b[0, i + 4]
        for k in range(1, group):
            value = value + adj_b[k, i + 4]
        dens[i] = slow[i + HALO - 1] * value
        return carry

    lax.fori_loop(0, rows + 2, density_row, 0, unroll=2)

    def smooth_row(i, carry):
        first, middle, last = (tiles_of(dens, (i + d,)) for d in range(3))
        value = {key: first[key] + 2.0 * middle[key] + last[key] for key in first}
        for beside in (beside_x, beside_z):
            low, high = beside(value, 0.0)
            value = {key: low[key] + 2.0 * value[key] + high[key] for key in value}
        for t, h in value:
            part[(i,) + at_tile(t, h)] = value[t, h] * (1.0 / 64.0)
        return carry

    lax.fori_loop(0, rows, smooth_row, 0, unroll=2)

    for i in range(peers):
        q = (m + i) % peers
        piece = part.at[:, pl.ds(pl.multiple_of(q * chunk_x, chunk_x), chunk_x), :]
        if i == 0:
            pltpu.make_async_copy(piece, parts.at[m], recv_sem.at[7]).start()
        else:
            pltpu.make_async_remote_copy(
                piece,
                parts.at[m],
                send_sem.at[7],
                recv_sem.at[7],
                device_id=(q * group + g, p),
                device_id_type=MESH,
            ).start()
    for k in range(1, group):
        send_times(k)
    pltpu.make_async_copy(parts, parts, recv_sem.at[7]).wait()
    summed = parts[0]
    for i in range(1, peers):
        summed = summed + parts[i]
    total[...] = summed
    place_k = block % per_owner
    for k in range(chunk_x):
        to = targets[k]
        piece = total.at[:, k, :]
        place = kernel_out.at[pl.ds(pl.multiple_of(place_k * rows, 8), rows), :]
        mine = (to[0] == s) & (to[1] == p)

        @pl.when(mine)
        def _():
            pltpu.make_async_copy(piece, place, recv_sem.at[8]).start()

        @pl.when(jnp.logical_not(mine))
        def _():
            pltpu.make_async_remote_copy(
                piece,
                place,
                last_sem.at[k],
                recv_sem.at[8],
                device_id=to,
                device_id_type=MESH,
            ).start()

    def drain(ref, sem):
        pltpu.make_async_copy(ref, ref, sem).wait()

    drain(velocity_ref.at[pl.ds(0, (n_space - 1) * rows), :], send_sem.at[0])
    drain(meta.at[0, pl.ds(0, n_space - 8), :], send_sem.at[1])
    for _ in range(7):
        drain(meta_ref, send_sem.at[1])
    for _ in partners:
        drain(delay.at[0], send_sem.at[2])
        drain(meta.at[0], send_sem.at[3])
    for halo in halos:
        halo.wait_send()
    for halo in event_halos:
        halo.wait_send()
    drain(times_out.at[pl.ds(0, (n_blocks - 1) * rows), :], send_sem.at[6])
    drain(parts.at[pl.ds(1, peers - 1)], send_sem.at[7])
    for k in range(chunk_x):
        to = targets[k]
        mine = (to[0] == s) & (to[1] == p)

        @pl.when(jnp.logical_not(mine))
        def _():
            drain(total.at[:, k, :], last_sem.at[k])

    drain(times_out, recv_sem.at[6])
    drain(kernel_out, recv_sem.at[8])


def per_device(dims, velocity, station_cells, event_cells, delays, active):
    n_src, n_space, ny, nz, events = dims
    rows = ny // (n_space * GROUP)
    tall = rows + 2 * HALO
    peers = n_src // GROUP
    chunk_x = n_space // peers
    own_rows = ny // n_src
    src_rows = rows + 10
    f32 = jnp.float32
    plane = (n_space, nz)
    smem = pl.BlockSpec(memory_space=pltpu.SMEM)
    anywhere = pl.BlockSpec(memory_space=pl.ANY)
    hbm = pl.BlockSpec(memory_space=pltpu.HBM)
    times, kernel_part = pl.pallas_call(
        functools.partial(kernel, dims),
        out_shape=(
            jax.ShapeDtypeStruct((ny, nz), f32),
            jax.ShapeDtypeStruct((own_rows, nz), f32),
        ),
        in_specs=[hbm, smem, smem, hbm, hbm],
        out_specs=(anywhere, anywhere),
        scratch_shapes=[
            pltpu.VMEM((1, 128), f32),
            pltpu.VMEM((3, events), jnp.int32),
            pltpu.VMEM((tall,) + plane, f32),
            pltpu.VMEM((tall,) + plane, f32),
            pltpu.VMEM((GROUP, n_space, 128), f32),
            pltpu.VMEM((GROUP, 1, events), f32),
            pltpu.VMEM((GROUP, tall + 2) + plane, f32),
            pltpu.VMEM((GROUP, tall + 2) + plane, f32),
            pltpu.VMEM((GROUP, tall + 2) + plane, f32),
            pltpu.VMEM((src_rows,) + plane, f32),
            pltpu.VMEM((src_rows, GROUP) + plane, f32),
            pltpu.VMEM((rows * n_space, events), jnp.bfloat16),
            pltpu.VMEM((2, GROUP, 3) + plane, f32),
            pltpu.VMEM((GROUP,) + plane, f32),
            pltpu.VMEM((GROUP, 6, src_rows - 2) + plane, f32),
            pltpu.VMEM((GROUP, src_rows) + plane, f32),
            pltpu.VMEM((GROUP, src_rows) + plane, f32),
            pltpu.VMEM((GROUP, src_rows) + plane, f32),
            pltpu.VMEM((rows + 2,) + plane, f32),
            pltpu.VMEM((rows,) + plane, f32),
            pltpu.VMEM((peers, rows, chunk_x, nz), f32),
            pltpu.VMEM((rows, chunk_x, nz), f32),
            pltpu.SemaphoreType.DMA,
            pltpu.SemaphoreType.DMA((8,)),
            pltpu.SemaphoreType.DMA((10,)),
            pltpu.SemaphoreType.DMA((4,)),
            pltpu.SemaphoreType.DMA((4,)),
            pltpu.SemaphoreType.DMA((4,)),
            pltpu.SemaphoreType.DMA((4,)),
            pltpu.SemaphoreType.DMA((chunk_x,)),
        ],
        compiler_params=pltpu.CompilerParams(
            collective_id=0, has_side_effects=True, vmem_limit_bytes=48 << 20
        ),
    )(
        *(
            pltpu.with_memory_space_constraint(array, pltpu.HBM)
            for array in (velocity[0], station_cells, active[:, 0, 0, :], event_cells, delays)
        )
    )
    return times[None, None], kernel_part[None]


def solution(mesh):
    n_src, n_space = mesh.shape["src"], mesh.shape["space"]

    def run(velocity, station_cells, event_cells, delays, active):
        dims = (n_src, n_space, velocity.shape[1], velocity.shape[2], event_cells.shape[1])
        return jax.shard_map(
            functools.partial(per_device, dims),
            mesh=mesh,
            in_specs=(
                P("space", None, None),
                P("src", None),
                P(),
                P("src", None),
                P(None, "src", "space", None),
            ),
            out_specs=(P("src", "space", None, None), P("space", "src", None)),
            check_vma=False,
        )(velocity, station_cells, event_cells, delays, active)

    return run
```

```python
import functools

import jax
import jax.numpy as jnp
from jax import lax
from jax.experimental import pallas as pl
from jax.experimental.pallas import tpu as pltpu
from jax.sharding import PartitionSpec as P

TY = 32
BIG = 1000000.0
HALO = 8
GROUP = 2
MESH = pl.DeviceIdType.MESH


def godunov(near_x, near_y, near_z, cost, cost_1, cost_2, cost_3):
    low_xy = jnp.minimum(near_x, near_y)
    high_xy = jnp.maximum(near_x, near_y)
    lowest = jnp.minimum(low_xy, near_z)
    rest = jnp.maximum(low_xy, near_z)
    gap2 = jnp.minimum(high_xy, rest) - lowest
    gap3 = jnp.maximum(high_xy, rest) - lowest
    step = gap3 - gap2
    spread = gap3 * gap3 + step * step
    two = cost_1 <= spread
    disc = jnp.where(two, cost_2, cost_3 - spread) - gap2 * gap2
    base = gap2 + jnp.where(two, 0.0, gap3)
    scale = jnp.where(two, 0.5, 1.0 / 3.0)
    disc = jnp.maximum(disc, 1e-30)
    wide = (base + disc * lax.rsqrt(disc)) * scale
    return lowest + jnp.where(cost <= gap2, cost, wide)


def tiles_of(ref, index):
    return {
        (t, h): ref[index + (pl.ds(8 * t, 8), pl.ds(128 * h, 128))]
        for t in range(ref.shape[-2] // 8)
        for h in range(ref.shape[-1] // 128)
    }


def at_tile(t, h):
    return (pl.ds(8 * t, 8), pl.ds(128 * h, 128))


def beside_x(field, fill):
    sub = lax.broadcasted_iota(jnp.int32, (8, 128), 0)
    down = {key: pltpu.roll(value, 1, 0) for key, value in field.items()}
    up = {key: pltpu.roll(value, 7, 0) for key, value in field.items()}
    low = {(t, h): jnp.where(sub == 0, down.get((t - 1, h), fill), down[t, h]) for t, h in field}
    high = {(t, h): jnp.where(sub == 7, up.get((t + 1, h), fill), up[t, h]) for t, h in field}
    return low, high


def beside_z(field, fill):
    lane = lax.broadcasted_iota(jnp.int32, (8, 128), 1)
    down = {key: pltpu.roll(value, 1, 1) for key, value in field.items()}
    up = {key: pltpu.roll(value, 127, 1) for key, value in field.items()}
    low = {(t, h): jnp.where(lane == 0, down.get((t, h - 1), fill), down[t, h]) for t, h in field}
    high = {(t, h): jnp.where(lane == 127, up.get((t, h + 1), fill), up[t, h]) for t, h in field}
    return low, high


def root(value):
    return value * lax.rsqrt(jnp.maximum(value, 1e-30))


def kernel(
    dims,
    velocity_ref,
    cells_ref,
    flags_ref,
    events_hbm,
    delays_ref,
    times_out,
    kernel_out,
    meta_ref,
    events_ref,
    vel,
    slow,
    meta,
    delay,
    start,
    time_a,
    time_b,
    count,
    landed,
    left,
    masks,
    spot,
    weights,
    source,
    adj_a,
    adj_b,
    dens,
    part,
    parts,
    total,
    local_sem,
    send_sem,
    recv_sem,
    halo_send,
    halo_recv,
    event_send,
    event_recv,
    last_sem,
):
    n_src, n_space, ny, nz, events = dims
    group = GROUP
    rows = ny // (n_space * group)
    peers = n_src // group
    chunk_x = n_space // peers
    own_rows = ny // n_src
    per_owner = own_rows // rows
    tall = rows + 2 * HALO
    s, p = lax.axis_index("src"), lax.axis_index("space")
    m, g = s // group, s % group
    block = g * n_space + p
    y_base = block * rows
    n_blocks = n_space * group

    def where_is(b):
        return (m * group + b // n_space, b % n_space)

    owner = block // per_owner
    targets = [(owner, chunk_x * m + k) for k in range(chunk_x)]
    sources = []
    for k in range(per_owner):
        b = s * per_owner + k
        sources.append(((p // chunk_x) * group + b // n_space, b % n_space))

    fetch_events = pltpu.make_async_copy(events_hbm, events_ref, local_sem)
    fetch_events.start()

    lane = lax.broadcasted_iota(jnp.int32, (1, 128), 1)
    line = jnp.zeros((1, 128), jnp.float32)
    tile_count = ny // TY
    for r in range(2):
        for t in range(tile_count):
            flag = flags_ref[r, t].astype(jnp.float32)
            line = jnp.where(lane == r * tile_count + t, flag, line)
    for d in range(3):
        line = jnp.where(lane == 64 + d, cells_ref[0, d].astype(jnp.float32), line)
    meta_ref[...] = line

    barrier = pltpu.get_barrier_semaphore()
    signals = 0
    for i in range(1, n_space):
        to = (s, (p + i) % n_space)
        pl.semaphore_signal(barrier, inc=1, device_id=to, device_id_type=MESH)
        signals += 1
    for dg in range(1, group):
        to = (m * group + (g + dg) % group, p)
        pl.semaphore_signal(barrier, inc=1, device_id=to, device_id_type=MESH)
        signals += 1
    for i in range(1, peers):
        to = (((m + i) % peers) * group + g, p)
        pl.semaphore_signal(barrier, inc=1, device_id=to, device_id_type=MESH)
        signals += 1
    for to in sources:
        mine = (to[0] == s) & (to[1] == p)

        @pl.when(jnp.logical_not(mine))
        def _():
            pl.semaphore_signal(barrier, inc=1, device_id=to, device_id_type=MESH)

        signals = signals + jnp.where(mine, 0, 1)

    src_rows = rows + 10
    cells = rows * n_space
    step_events = 4096
    steps = events // step_events
    contract = (((1,), (1,)), ((), ()))
    mine_rows = pl.ds(5, rows)
    count[mine_rows] = jnp.zeros((rows, n_space, nz), jnp.float32)
    fetch_events.wait()

    def product(first, second):
        out = lax.dot_general(first, second, contract, preferred_element_type=jnp.float32)
        return out.reshape(rows, n_space, nz)

    def depth_of(at):
        deep = lax.broadcasted_iota(jnp.int32, (nz, step_events), 0)
        return deep == events_ref[2:3, at]

    def count_events(c, carry):
        at = pl.ds(pl.multiple_of(c * step_events, step_events), step_events)
        key = (events_ref[1:2, at] - y_base) * n_space + events_ref[0:1, at]
        cell = lax.broadcasted_iota(jnp.int32, (cells, step_events), 0)
        left[:, at] = jnp.where(cell == key, 1.0, 0.0).astype(jnp.bfloat16)
        right = jnp.where(depth_of(at), 1.0, 0.0).astype(jnp.bfloat16)
        count[mine_rows] += product(left[:, at], right)
        return carry

    lax.fori_loop(0, steps, count_events, 0)
    pl.semaphore_wait(barrier, signals)

    own = pl.ds(HALO, rows)
    partners = [(m * group + (g + dg) % group, p) for dg in range(1, group)]
    for i in range(n_space):
        q = (p + i) % n_space
        line = meta.at[g, pl.ds(p, 1), :]
        if i == 0:
            pltpu.make_async_copy(meta_ref, line, recv_sem.at[1]).start()
        else:
            pltpu.make_async_remote_copy(
                meta_ref,
                line,
                send_sem.at[1],
                recv_sem.at[1],
                device_id=(s, q),
                device_id_type=MESH,
            ).start()
    half = n_space // 2
    near_half = (p // half) * half
    far_half = half - near_half
    for i in range(n_space):
        if i < half:
            q = near_half + (p + i) % half
        else:
            q = far_half + (p + i) % half
        piece = velocity_ref.at[pl.ds(pl.multiple_of((g * n_space + q) * rows, 8), rows), :]
        arrived = recv_sem.at[0] if i < half else recv_sem.at[9]
        if i == 0:
            pltpu.make_async_copy(piece, vel.at[own, p, :], arrived).start()
        else:
            pltpu.make_async_remote_copy(
                piece,
                vel.at[own, p, :],
                send_sem.at[0],
                arrived,
                device_id=(s, q),
                device_id_type=MESH,
            ).start()
    pltpu.make_async_copy(delays_ref, delay.at[g], recv_sem.at[2]).start()
    for to in partners:
        pltpu.make_async_remote_copy(
            delays_ref,
            delay.at[g],
            send_sem.at[2],
            recv_sem.at[2],
            device_id=to,
            device_id_type=MESH,
        ).start()

    before = where_is((block + n_blocks - 1) % n_blocks)
    after = where_is((block + 1) % n_blocks)

    def event_halo(ref, n, to):
        at, there = ((5, 5 + rows), (rows, 0))[n % 2]
        return pltpu.make_async_remote_copy(
            ref.at[pl.ds(at, 5)],
            ref.at[pl.ds(there, 5)],
            event_send.at[n],
            event_recv.at[n],
            device_id=to,
            device_id_type=MESH,
        )

    pltpu.make_async_copy(delay, delay, recv_sem.at[2]).wait()
    event_halos = [event_halo(count, 0, before), event_halo(count, 1, after)]
    for halo in event_halos:
        halo.start()

    landed[mine_rows] = jnp.zeros((rows, group, n_space, nz), jnp.float32)

    def add_events(c, carry):
        at = pl.ds(pl.multiple_of(c * step_events, step_events), step_events)
        deep = depth_of(at)
        for k in range(group):
            lateness = delay[k, 0:1, at]
            coarse = lateness.astype(jnp.bfloat16).astype(jnp.float32)
            sums = [
                product(left[:, at], jnp.where(deep, value, 0.0).astype(jnp.bfloat16))
                for value in (coarse, lateness - coarse)
            ]
            landed[mine_rows, k] += sums[0] + sums[1]
        return carry

    wide_lane = lax.broadcasted_iota(jnp.int32, (n_space, 128), 1)
    layer_f = lax.broadcasted_iota(jnp.int32, (n_space, nz), 0).astype(jnp.float32)
    depth_f = lax.broadcasted_iota(jnp.int32, (n_space, nz), 1).astype(jnp.float32)
    first_tile = (y_base - HALO + TY) // TY - 1

    def column(k, index):
        picked = jnp.where(wide_lane == index, meta[k], 0.0)
        return jnp.broadcast_to(jnp.sum(picked, axis=1, keepdims=True), (n_space, nz))

    def row_valid(y):
        return (y >= 0) & (y < ny)

    def init_fields():
        for dg in range(1, group):
            other = (g + dg) % group
            pltpu.make_async_copy(meta.at[other], meta.at[other], recv_sem.at[3]).wait()
        for k in range(group):
            for r in range(2):
                for t in range(2):
                    masks[r, k, t] = column(k, r * tile_count + first_tile + t)
                masks[r, k, 2] = jnp.zeros((n_space, nz), jnp.float32)
            cell_x, cell_y, cell_z = column(k, 64), column(k, 65), column(k, 66)
            here = (layer_f == cell_x) & (depth_f == cell_z)
            spot[k] = jnp.where(here, cell_y, -1.0)
            off_x, off_z = layer_f - cell_x, depth_f - cell_z
            flat = off_x * off_x + off_z * off_z

            def init_row(j, carry):
                y = y_base - HALO - 1 + j
                diff = y.astype(jnp.float32) - cell_y
                start[k, j] = jnp.where(row_valid(y), root(flat + diff * diff), BIG)
                return carry

            lax.fori_loop(0, tall + 2, init_row, 0, unroll=4)

    cut = steps // 2
    lax.fori_loop(0, cut, add_events, 0)

    pltpu.make_async_copy(meta.at[g], meta.at[g], recv_sem.at[1]).wait()
    for to in partners:
        pltpu.make_async_remote_copy(
            meta.at[g],
            meta.at[g],
            send_sem.at[3],
            recv_sem.at[3],
            device_id=to,
            device_id_type=MESH,
        ).start()
    lax.fori_loop(cut, steps, add_events, 0)

    halos = []
    for n, (x_at, arrived) in enumerate(((near_half, 0), (far_half, 9))):
        layers = pl.ds(pl.multiple_of(x_at, half), half)
        here = vel.at[own, layers, :]
        pltpu.make_async_copy(here, here, recv_sem.at[arrived]).wait()
        for d, (at, there, to) in enumerate(
            ((HALO, HALO + rows, before), (rows, 0, after))
        ):
            halo = pltpu.make_async_remote_copy(
                vel.at[pl.ds(at, HALO), layers, :],
                vel.at[pl.ds(there, HALO), layers, :],
                halo_send.at[2 * n + d],
                halo_recv.at[2 * n + d],
                device_id=to,
                device_id_type=MESH,
            )
            halo.start()
            halos.append(halo)

    for n, to in ((2, before), (3, after)):
        halo = event_halo(landed, n, to)
        halo.start()
        event_halos.append(halo)

    init_fields()

    def slow_row(j, carry):
        slow[j] = 1.0 / vel[j]
        return carry

    def sweep_row(old, new, r, j):
        y = y_base - HALO + j
        kind = jnp.where(row_valid(y), (y + TY) // TY - 1 - first_tile, 2)
        level = y.astype(jnp.float32)
        centre = [tiles_of(old, (k, j + 1)) for k in range(group)]
        near_x = [beside_x(field, BIG) for field in centre]
        near_z = [beside_z(field, BIG) for field in centre]
        for t, h in centre[0]:
            tile = at_tile(t, h)
            cost = slow[(j,) + tile]
            cost_1 = cost * cost
            cost_2 = cost_1 + cost_1
            cost_3 = cost_2 + cost_1
            for k in range(group):
                update = godunov(
                    jnp.minimum(near_x[k][0][t, h], near_x[k][1][t, h]),
                    jnp.minimum(old[(k, j) + tile], old[(k, j + 2) + tile]),
                    jnp.minimum(near_z[k][0][t, h], near_z[k][1][t, h]),
                    cost,
                    cost_1,
                    cost_2,
                    cost_3,
                )
                chosen = (masks[(r, k, kind) + tile] > 0.0) & (spot[(k,) + tile] != level)
                new[(k, j + 1) + tile] = jnp.where(chosen, update, centre[k][t, h])

    stages = ((start, time_a, 0), (time_a, time_b, 0), (time_b, time_a, 1), (time_a, time_b, 1))
    lax.fori_loop(HALO, HALO + rows, slow_row, 0, unroll=4)
    for n, (old, new, r) in enumerate(stages):

        def inside(j, carry):
            sweep_row(old, new, r, j)
            return carry

        lax.fori_loop(HALO + n, HALO + rows - n, inside, 0, unroll=2)

    for halo in halos:
        halo.wait_recv()
    lax.fori_loop(0, HALO, slow_row, 0, unroll=4)
    lax.fori_loop(HALO + rows, tall, slow_row, 0, unroll=4)
    for n, (old, new, r) in enumerate(stages):

        def outside(i, carry):
            sweep_row(old, new, r, n + i)
            sweep_row(old, new, r, HALO + rows - n + i)
            return carry

        lax.fori_loop(0, HALO, outside, 0, unroll=4)

    inner = pl.ds(HALO + 1, rows)

    def send_times(k):
        for i in range(n_space):
            q = (p + i) % n_space
            piece = time_b.at[k, inner, q, :]
            place = times_out.at[pl.ds(pl.multiple_of(y_base, 8), rows), :]
            to_src = m * group + k

            def send(piece=piece, place=place, to_src=to_src, q=q):
                pltpu.make_async_remote_copy(
                    piece,
                    place,
                    send_sem.at[6],
                    recv_sem.at[6],
                    device_id=(to_src, q),
                    device_id_type=MESH,
                ).start()

            if i:
                send()
            else:

                @pl.when(g == k)
                def _():
                    pltpu.make_async_copy(piece, place, recv_sem.at[6]).start()

                @pl.when(g != k)
                def _():
                    send()

    send_times(0)

    def weight_row(i, carry):
        j = i + 5
        for k in range(group):
            centre = tiles_of(time_b, (k, j))
            x_low, x_high = beside_x(centre, 0.0)
            z_low, z_high = beside_z(centre, 0.0)
            for t, h in centre:
                tile = at_tile(t, h)
                rate = vel[(i + 4,) + tile] * (1.0 / 6.0)
                around = (
                    x_low[t, h],
                    x_high[t, h],
                    time_b[(k, j - 1) + tile],
                    time_b[(k, j + 1) + tile],
                    z_low[t, h],
                    z_high[t, h],
                )
                for d, near in enumerate(around):
                    weights[(k, d, i) + tile] = jnp.maximum(near - centre[t, h], 0.0) * rate
        return carry

    lax.fori_loop(0, src_rows - 2, weight_row, 0, unroll=4)

    for halo in event_halos:
        halo.wait_recv()

    def source_row(i, carry):
        valid = row_valid(y_base - 5 + i)
        for k in range(group):
            shift = time_b[k, i + 4] - start[k, i + 4]
            value = count[i] * shift - landed[i, k]
            source[k, i] = jnp.where(valid, value, 0.0)
        return carry

    lax.fori_loop(0, src_rows, source_row, 0, unroll=2)

    def adjoint_sweep(old, new, low, high):
        def row(i, carry):
            for k in range(group):
                centre = tiles_of(old, (k, i))
                x_low, x_high = beside_x(centre, 0.0)
                z_low, z_high = beside_z(centre, 0.0)
                for t, h in centre:
                    tile = at_tile(t, h)
                    weight = [weights[(k, d, i - 1) + tile] for d in range(6)]
                    along_x = weight[0] * x_low[t, h] + weight[1] * x_high[t, h]
                    along_y = weight[2] * old[(k, i - 1) + tile] + weight[3] * old[(k, i + 1) + tile]
                    along_z = weight[4] * z_low[t, h] + weight[5] * z_high[t, h]
                    new[(k, i) + tile] = source[(k, i) + tile] + along_x + (along_y + along_z)
            return carry

        lax.fori_loop(low, high, row, 0, unroll=4)

    adjoint_sweep(source, adj_a, 1, src_rows - 1)
    adjoint_sweep(adj_a, adj_b, 2, src_rows - 2)
    adjoint_sweep(adj_b, adj_a, 3, src_rows - 3)
    adjoint_sweep(adj_a, adj_b, 4, src_rows - 4)

    def density_row(i, carry):
        value = adj_b[0, i + 4]
        for k in range(1, group):
            value = value + adj_b[k, i + 4]
        dens[i] = slow[i + HALO - 1] * value
        return carry

    lax.fori_loop(0, rows + 2, density_row, 0, unroll=2)

    def smooth_row(i, carry):
        first, middle, last = (tiles_of(dens, (i + d,)) for d in range(3))
        value = {key: first[key] + 2.0 * middle[key] + last[key] for key in first}
        for beside in (beside_x, beside_z):
            low, high = beside(value, 0.0)
            value = {key: low[key] + 2.0 * value[key] + high[key] for key in value}
        for t, h in value:
            part[(i,) + at_tile(t, h)] = value[t, h] * (1.0 / 64.0)
        return carry

    lax.fori_loop(0, rows, smooth_row, 0, unroll=2)

    for i in range(peers):
        q = (m + i) % peers
        piece = part.at[:, pl.ds(pl.multiple_of(q * chunk_x, chunk_x), chunk_x), :]
        if i == 0:
            pltpu.make_async_copy(piece, parts.at[m], recv_sem.at[7]).start()
        else:
            pltpu.make_async_remote_copy(
                piece,
                parts.at[m],
                send_sem.at[7],
                recv_sem.at[7],
                device_id=(q * group + g, p),
                device_id_type=MESH,
            ).start()
    for k in range(1, group):
        send_times(k)
    pltpu.make_async_copy(parts, parts, recv_sem.at[7]).wait()
    summed = parts[0]
    for i in range(1, peers):
        summed = summed + parts[i]
    total[...] = summed
    place_k = block % per_owner
    for k in range(chunk_x):
        to = targets[k]
        piece = total.at[:, k, :]
        place = kernel_out.at[pl.ds(pl.multiple_of(place_k * rows, 8), rows), :]
        mine = (to[0] == s) & (to[1] == p)

        @pl.when(mine)
        def _():
            pltpu.make_async_copy(piece, place, recv_sem.at[8]).start()

        @pl.when(jnp.logical_not(mine))
        def _():
            pltpu.make_async_remote_copy(
                piece,
                place,
                last_sem.at[k],
                recv_sem.at[8],
                device_id=to,
                device_id_type=MESH,
            ).start()

    def drain(ref, sem):
        pltpu.make_async_copy(ref, ref, sem).wait()

    drain(velocity_ref.at[pl.ds(0, (n_space - 1) * rows), :], send_sem.at[0])
    drain(meta.at[0, pl.ds(0, n_space - 8), :], send_sem.at[1])
    for _ in range(7):
        drain(meta_ref, send_sem.at[1])
    for _ in partners:
        drain(delay.at[0], send_sem.at[2])
        drain(meta.at[0], send_sem.at[3])
    for halo in halos:
        halo.wait_send()
    for halo in event_halos:
        halo.wait_send()
    drain(times_out.at[pl.ds(0, (n_blocks - 1) * rows), :], send_sem.at[6])
    drain(parts.at[pl.ds(1, peers - 1)], send_sem.at[7])
    for k in range(chunk_x):
        to = targets[k]
        mine = (to[0] == s) & (to[1] == p)

        @pl.when(jnp.logical_not(mine))
        def _():
            drain(total.at[:, k, :], last_sem.at[k])

    drain(times_out, recv_sem.at[6])
    drain(kernel_out, recv_sem.at[8])


def per_device(dims, velocity, station_cells, event_cells, delays, active):
    n_src, n_space, ny, nz, events = dims
    rows = ny // (n_space * GROUP)
    tall = rows + 2 * HALO
    peers = n_src // GROUP
    chunk_x = n_space // peers
    own_rows = ny // n_src
    src_rows = rows + 10
    f32 = jnp.float32
    plane = (n_space, nz)
    smem = pl.BlockSpec(memory_space=pltpu.SMEM)
    anywhere = pl.BlockSpec(memory_space=pl.ANY)
    hbm = pl.BlockSpec(memory_space=pltpu.HBM)
    times, kernel_part = pl.pallas_call(
        functools.partial(kernel, dims),
        out_shape=(
            jax.ShapeDtypeStruct((ny, nz), f32),
            jax.ShapeDtypeStruct((own_rows, nz), f32),
        ),
        in_specs=[hbm, smem, smem, hbm, hbm],
        out_specs=(anywhere, anywhere),
        scratch_shapes=[
            pltpu.VMEM((1, 128), f32),
            pltpu.VMEM((3, events), jnp.int32),
            pltpu.VMEM((tall,) + plane, f32),
            pltpu.VMEM((tall,) + plane, f32),
            pltpu.VMEM((GROUP, n_space, 128), f32),
            pltpu.VMEM((GROUP, 1, events), f32),
            pltpu.VMEM((GROUP, tall + 2) + plane, f32),
            pltpu.VMEM((GROUP, tall + 2) + plane, f32),
            pltpu.VMEM((GROUP, tall + 2) + plane, f32),
            pltpu.VMEM((src_rows,) + plane, f32),
            pltpu.VMEM((src_rows, GROUP) + plane, f32),
            pltpu.VMEM((rows * n_space, events), jnp.bfloat16),
            pltpu.VMEM((2, GROUP, 3) + plane, f32),
            pltpu.VMEM((GROUP,) + plane, f32),
            pltpu.VMEM((GROUP, 6, src_rows - 2) + plane, f32),
            pltpu.VMEM((GROUP, src_rows) + plane, f32),
            pltpu.VMEM((GROUP, src_rows) + plane, f32),
            pltpu.VMEM((GROUP, src_rows) + plane, f32),
            pltpu.VMEM((rows + 2,) + plane, f32),
            pltpu.VMEM((rows,) + plane, f32),
            pltpu.VMEM((peers, rows, chunk_x, nz), f32),
            pltpu.VMEM((rows, chunk_x, nz), f32),
            pltpu.SemaphoreType.DMA,
            pltpu.SemaphoreType.DMA((8,)),
            pltpu.SemaphoreType.DMA((10,)),
            pltpu.SemaphoreType.DMA((4,)),
            pltpu.SemaphoreType.DMA((4,)),
            pltpu.SemaphoreType.DMA((4,)),
            pltpu.SemaphoreType.DMA((4,)),
            pltpu.SemaphoreType.DMA((chunk_x,)),
        ],
        compiler_params=pltpu.CompilerParams(
            collective_id=0, has_side_effects=True, vmem_limit_bytes=48 << 20
        ),
    )(
        *(
            pltpu.with_memory_space_constraint(array, pltpu.HBM)
            for array in (velocity[0], station_cells, active[:, 0, 0, :], event_cells, delays)
        )
    )
    return times[None, None], kernel_part[None]


def solution(mesh):
    n_src, n_space = mesh.shape["src"], mesh.shape["space"]

    def run(velocity, station_cells, event_cells, delays, active):
        dims = (n_src, n_space, velocity.shape[1], velocity.shape[2], event_cells.shape[1])
        return jax.shard_map(
            functools.partial(per_device, dims),
            mesh=mesh,
            in_specs=(
                P("space", None, None),
                P("src", None),
                P(),
                P("src", None),
                P(None, "src", "space", None),
            ),
            out_specs=(P("src", "space", None, None), P("space", "src", None)),
            check_vma=False,
        )(velocity, station_cells, event_cells, delays, active)

    return run
```
